128 devices in a mesh: row: 8 (over x, core), col: 16 (over y, z).
Axes of the slice: x: 4, y: 4, z: 4, core: 2. Of those that a mesh axis runs over, the one named last changes fastest.
Arguments:
- series: bfloat16 [512, 32768], P(None, ('row', 'col')), may hold values from -6 to 6
- lag_weight: float32 [4], replicated, may hold values from 0.25 to 1
- start_basis: bfloat16 [64, 32768], P(None, ('row', 'col')), may hold values from -5.25 to 5.25
- block_pairs: int32 [8, 16, 32, 2], P('row', 'col'), may hold values from 0 to 127, as said below
- pair_count: int32 [8, 16], P('row', 'col'), may hold values from 1 to 32, as said below
Outputs:
- basis: float32 [64, 32768], P(None, ('row', 'col'))
- rayleigh: float32 [64, 64], replicated
The draws below stay inside these ranges and needn't reach their ends.
Inputs may be any that keep to these rules, and one draw needn't show every extreme that they name: For every slot s of device (r, c), block_pairs[r, c, s, 0] is a block of row group r, from r * 16 to (r + 1) * 16 - 1, and block_pairs[r, c, s, 1] is a block held by a device of mesh column c: (block_pairs[r, c, s, 1]) mod (16) equals c. Slots that are not live hold blocks of the same ranges and are no part of the network. `pair_count`: the number of live slots of device (r, c); some device has exactly 32.
All inputs are finite; a program needn't handle non-finite values.
Results may differ from the reference program's by a relative error of at most 0.0045.
Values may be sent and summed in bfloat16 or wider, within the bound.
No kernel may reach another device: no remote copies, remote signals or barrier semaphores. Data moves between devices by JAX's collectives and lax.ppermute only.
A program may use at most 64 MiB of HBM per device.

```python
import math
import jax
import jax.numpy as jnp
from jax import lax

BLOCK = 256
DAYS = 512
LAGS = 4
RANK = 64
ITERS = 2
BLK_DEV = 1
SLOTS = 32
CELLS = 32768
N_ROW = 8
N_COL = 16


def draw_block_pairs(key, part):
    lead_key = jax.random.fold_in(key, 11)
    trail_key = jax.random.fold_in(key, 13)
    within_key = jax.random.fold_in(key, 17)
    shape_all = (N_ROW, N_COL, SLOTS)
    row_groups = jnp.arange(N_ROW, dtype=jnp.int32).reshape(N_ROW, 1, 1)
    col_groups = jnp.arange(N_COL, dtype=jnp.int32).reshape(1, N_COL, 1)
    lead_ids = row_groups * (BLK_DEV * N_COL) + jax.random.randint(lead_key, shape_all, 0, BLK_DEV * N_COL)
    trail_rows = jax.random.randint(trail_key, shape_all, 0, N_ROW)
    trail_ids = (trail_rows * N_COL + col_groups) * BLK_DEV + jax.random.randint(within_key, shape_all, 0, BLK_DEV)
    return jnp.stack([lead_ids, trail_ids], axis=-1).astype(jnp.int32)


def draw_pair_count(key, part):
    first_key = jax.random.fold_in(key, 7)
    second_key = jax.random.fold_in(key, 9)
    chosen_key = jax.random.fold_in(key, 19)
    device_total = N_ROW * N_COL
    first_draw = jax.random.randint(first_key, (device_total,), 1, SLOTS + 1)
    second_draw = jax.random.randint(second_key, (device_total,), 1, SLOTS + 1)
    counts = jnp.maximum(1, first_draw * second_draw // SLOTS)
    chosen = jax.random.randint(chosen_key, (), 0, device_total)
    counts = jnp.where(jnp.arange(device_total) == chosen, SLOTS, counts)
    return counts.reshape(N_ROW, N_COL).astype(jnp.int32)


def draw_start_basis(key, part):
    sign_key = jax.random.fold_in(key, 23)
    strength_key = jax.random.fold_in(key, 29)
    shared_key = jax.random.fold_in(key, 31)
    own_key = jax.random.fold_in(key, 37)
    signs = jnp.where(jax.random.randint(sign_key, (RANK, 1), 0, 2) == 0, -1.0, 1.0).astype(jnp.float32)
    strength = jax.random.uniform(strength_key, (RANK, 1), jnp.float32, 0.8, 1.6)
    shared = jnp.clip(jax.random.normal(shared_key, (1, CELLS), jnp.float32), -3.0, 3.0)
    own = 0.05 * jnp.clip(jax.random.normal(own_key, (RANK, CELLS), jnp.float32), -6.0, 6.0)
    return (signs * strength * shared + own).astype(jnp.bfloat16)


def level_of(key, extent, pieces, low, largest):
    def one(dim, parts):
        heights = jax.random.uniform(jax.random.fold_in(jax.random.fold_in(key, 6), dim), (parts,), jnp.float32, low / len(pieces), largest / len(pieces))
        return jnp.repeat(jnp.exp(heights), extent[dim] // parts).reshape((-1,) + (1,) * (len(extent) - dim - 1))

    gain = one(*pieces[0])
    for cut in pieces[1:]:
        gain = gain * one(*cut)
    return gain


def centred(key, extent, spread, most, split=(), kind=jnp.bfloat16):
    result = jax.random.normal(key, extent, jnp.float32) * spread
    if len(split) > 0:
        result = level_of(key, extent, split, -0.22, 0.18) * result
    return jnp.clip(result, min=-most, max=most).astype(kind)


def setup_inputs(seed: int = 0) -> dict:
    keys = jax.random.split(jax.random.key(seed), 6)
    series = centred(keys[0], (DAYS, CELLS), 1.0, 6.0, ((1, 128),))
    lag_weight = jnp.clip(jnp.exp(jax.random.uniform(keys[1], (LAGS,), jnp.float32, math.log(0.25), math.log(1.0))), 0.25, 1.0)
    start_basis = draw_start_basis(jax.random.fold_in(keys[5], 71), 0)
    block_pairs = draw_block_pairs(jax.random.fold_in(keys[5], 71), 0)
    pair_count = draw_pair_count(jax.random.fold_in(keys[5], 71), 0)
    return {"series": series, "lag_weight": lag_weight, "start_basis": start_basis, "block_pairs": block_pairs, "pair_count": pair_count}


BETA_CORR = 8.0
GRAM_EPS = 1e-05
HIGHEST = lax.Precision.HIGHEST

def lagged_tile(lead_block, trail_block, lag_weight, tile_scale):
    day_count = lead_block.shape[0]
    block_width = lead_block.shape[1]
    lag_count = lag_weight.shape[0]
    zero_rows = jnp.zeros((lag_count, block_width), lead_block.dtype)
    lead_padded = jnp.concatenate([lead_block, zero_rows], axis=0)
    trail_padded = jnp.concatenate([trail_block, zero_rows], axis=0)
    lead_shifted = jnp.concatenate([lead_padded[offset:offset + day_count] for offset in range(lag_count)], axis=1)
    trail_shifted = jnp.concatenate([trail_padded[offset:offset + day_count] for offset in range(lag_count)], axis=1)
    contract = (((0,), (0,)), ((), ()))
    forward = lax.dot_general(lead_shifted, trail_block, contract, precision=HIGHEST)
    backward = lax.dot_general(lead_block, trail_shifted, contract, precision=HIGHEST)
    forward = forward.reshape(lag_count, block_width, block_width)
    backward = jnp.transpose(backward.reshape(block_width, lag_count, block_width), (1, 0, 2))
    soft_corr = jnp.tanh(BETA_CORR / day_count * (forward + backward))
    weighted = lax.optimization_barrier(jnp.sum(lag_weight[:, None, None] * soft_corr, axis=0))
    return (tile_scale * weighted).astype(jnp.bfloat16)

def network_product(basis_bf, series_full, lag_weight, block_pairs, pair_count):
    basis_full = basis_bf.astype(jnp.float32)
    slot_total = block_pairs.shape[2]
    lead_ids = block_pairs[:, :, :, 0].reshape(-1).astype(jnp.int32)
    trail_ids = block_pairs[:, :, :, 1].reshape(-1).astype(jnp.int32)
    alive = (jnp.arange(slot_total, dtype=jnp.int32)[None, :] < pair_count.reshape(-1, 1)).reshape(-1)
    tile_scale = 0.25 / math.sqrt(BLOCK)

    def one_slot(product, item):
        lead_id, trail_id, slot_alive = item
        lead_start = (lead_id * BLOCK).astype(jnp.int32)
        trail_start = (trail_id * BLOCK).astype(jnp.int32)

        def added(total):
            lead_block = lax.dynamic_slice_in_dim(series_full, lead_start, BLOCK, 1)
            trail_block = lax.dynamic_slice_in_dim(series_full, trail_start, BLOCK, 1)
            tile = lagged_tile(lead_block, trail_block, lag_weight, tile_scale).astype(jnp.float32)
            lead_basis = lax.dynamic_slice_in_dim(basis_full, lead_start, BLOCK, 1)
            trail_basis = lax.dynamic_slice_in_dim(basis_full, trail_start, BLOCK, 1)
            into_rows = jnp.dot(trail_basis, tile.T, precision=HIGHEST)
            into_cols = jnp.dot(lead_basis, tile, precision=HIGHEST)
            current = lax.dynamic_slice_in_dim(total, lead_start, BLOCK, 1)
            total = lax.dynamic_update_slice_in_dim(total, current + into_rows, lead_start, 1)
            current = lax.dynamic_slice_in_dim(total, trail_start, BLOCK, 1)
            return lax.dynamic_update_slice_in_dim(total, current + into_cols, trail_start, 1)
        return (lax.cond(slot_alive, added, lambda total: total, product), None)
    initial = jnp.zeros((RANK, CELLS), jnp.float32)
    product, ignored = lax.scan(one_slot, initial, (lead_ids, trail_ids, alive))
    return product

def orthonormal(product):
    gram = jnp.dot(product, product.T, precision=HIGHEST) / CELLS + GRAM_EPS * jnp.eye(RANK, dtype=jnp.float32)
    lower = jnp.linalg.cholesky(gram)
    return lax.linalg.triangular_solve(lower, product, left_side=True, lower=True)

def reference(series, lag_weight, start_basis, block_pairs, pair_count):
    series_full = series.astype(jnp.float32)
    current = start_basis
    basis = start_basis.astype(jnp.float32)
    for iteration in range(ITERS):
        product = network_product(current, series_full, lag_weight, block_pairs, pair_count)
        basis = orthonormal(product)
        current = basis.astype(jnp.bfloat16)
    final = network_product(current, series_full, lag_weight, block_pairs, pair_count)
    rayleigh = jnp.dot(final, current.astype(jnp.float32).T, precision=HIGHEST) / CELLS
    return (basis, rayleigh)
```

```python
import functools

import jax
import jax.numpy as jnp
from jax import lax
from jax.experimental import pallas as pl
from jax.experimental.pallas import tpu as pltpu
from jax.sharding import PartitionSpec as P

BLOCK = 256
DAYS = 512
LAGS = 4
RANK = 64
SLOTS = 32
N_ROW = 8
N_COL = 16
CELLS = 32768
BETA_CORR = 8.0
GRAM_EPS = 1e-05
TILE_SCALE = 0.25 / 16.0
HIGHEST = lax.Precision.HIGHEST
F32 = jnp.float32
BF16 = jnp.bfloat16
VMEM = pl.BlockSpec(memory_space=pltpu.VMEM)
SMEM = pl.BlockSpec(memory_space=pltpu.SMEM)


def call(body, out_shape, in_specs, flops, nbytes, scratch=(), name=None):
    many = isinstance(out_shape, (list, tuple))
    return pl.pallas_call(
        body,
        out_shape=out_shape,
        in_specs=in_specs,
        out_specs=[VMEM] * len(out_shape) if many else VMEM,
        scratch_shapes=list(scratch),
        compiler_params=pltpu.CompilerParams(vmem_limit_bytes=56 << 20),
        cost_estimate=pl.CostEstimate(flops=flops, bytes_accessed=nbytes, transcendentals=0),
        name=name,
    )


def shape(*dims, dtype=F32):
    return jax.ShapeDtypeStruct(dims, dtype)


def shift_body(b_ref, out_ref):
    def one(block, carry):
        x = b_ref[block].astype(F32)
        day = lax.broadcasted_iota(jnp.int32, (DAYS, BLOCK), 0)
        out_ref[block, 0] = (x + x).astype(BF16)
        for lag in range(1, LAGS):
            later = jnp.where(day < DAYS - lag, pltpu.roll(x, DAYS - lag, 0), 0.0)
            earlier = jnp.where(day >= lag, pltpu.roll(x, lag, 0), 0.0)
            out_ref[block, lag] = (later + earlier).astype(BF16)
        return carry

    lax.fori_loop(0, N_ROW, one, 0)


def day_sums(col_series):
    return call(
        shift_body,
        shape(N_ROW, LAGS, DAYS, BLOCK, dtype=BF16),
        [VMEM],
        10_000_000,
        10 << 20,
        name="day_sums",
    )(col_series)


def build_body(pairs, count, weight, at_ref, sums_ref, xr_ref, xc_ref, tiles_ref, rows_ref, cols_ref):
    rows_ref[...] = jnp.zeros_like(rows_ref)
    cols_ref[...] = jnp.zeros_like(cols_ref)

    def one(slot, carry):
        i = pairs[2 * slot] % N_COL
        j = pairs[2 * slot + 1] // N_COL
        lead = at_ref[i]
        total = None
        for lag in range(LAGS):
            lagged = jnp.dot(lead, sums_ref[j, lag], preferred_element_type=F32)
            term = weight[lag] * jnp.tanh(lagged * (BETA_CORR / DAYS))
            total = term if total is None else total + term
        tile = (total * TILE_SCALE).astype(BF16)
        tiles_ref[slot] = tile
        cols_ref[j] += jnp.dot(xr_ref[i], tile, preferred_element_type=F32)
        rows_ref[i] += lax.dot_general(
            xc_ref[j], tile, (((1,), (1,)), ((), ())), preferred_element_type=F32
        )
        return carry

    lax.fori_loop(0, count[0], one, 0)


def build(pairs, count, weight, at, sums, xr, xc):
    return call(
        build_body,
        [
            shape(SLOTS, BLOCK, BLOCK, dtype=BF16),
            shape(N_COL, RANK, BLOCK),
            shape(N_ROW, RANK, BLOCK),
        ],
        [SMEM, SMEM, SMEM, VMEM, VMEM, VMEM, VMEM],
        9_000_000_000,
        20 << 20,
        name="build",
    )(pairs, count, weight, at, sums, xr, xc)


def total_of(rr_ref, cc_ref):
    total = rr_ref[0] + cc_ref[0, :RANK]
    for k in range(1, N_COL):
        total = total + rr_ref[k]
    for k in range(1, N_ROW):
        total = total + cc_ref[k, :RANK]
    return total


def mid1_body(rr_ref, cc_ref, out_ref):
    total = total_of(rr_ref, cc_ref)
    high = total.astype(BF16)
    out_ref[:RANK] = high
    out_ref[RANK:] = (total - high.astype(F32)).astype(BF16)


def mid1(rr, cc):
    return call(mid1_body, shape(2 * RANK, BLOCK, dtype=BF16), [VMEM, VMEM], 1_000_000, 2 << 20, name="mid1")(rr, cc)


def product_body(pairs, count, tiles_ref, qr_ref, qc_ref, rows_ref, cols_ref):
    rows_ref[...] = jnp.zeros_like(rows_ref)
    cols_ref[...] = jnp.zeros_like(cols_ref)

    def one(slot, carry):
        i = pairs[2 * slot] % N_COL
        j = pairs[2 * slot + 1] // N_COL
        tile = tiles_ref[slot]
        into_cols = jnp.dot(qr_ref[i], tile, preferred_element_type=F32)
        into_rows = lax.dot_general(
            qc_ref[j], tile, (((1,), (1,)), ((), ())), preferred_element_type=F32
        )
        cols_ref[j, :RANK] += into_cols[:RANK] + into_cols[RANK:]
        rows_ref[i] += into_rows[:RANK] + into_rows[RANK:]
        return carry

    lax.fori_loop(0, count[0], one, 0)
    gram = jnp.zeros((RANK, RANK), F32)
    for k in range(N_COL):
        both = lax.dot_general(
            qr_ref[k, :RANK], qr_ref[k], (((1,), (1,)), ((), ())), preferred_element_type=F32
        )
        low_high = lax.dot_general(
            qr_ref[k, RANK:], qr_ref[k, :RANK], (((1,), (1,)), ((), ())), preferred_element_type=F32
        )
        gram = gram + both[:, :RANK] + (both[:, RANK:] + low_high)
    for k in range(N_ROW):
        for q in range(4):
            cols_ref[k, RANK:, 64 * q : 64 * q + 64] = gram[16 * q : 16 * q + 16]


def product(pairs, count, tiles, qr, qc):
    return call(
        product_body,
        [shape(N_COL, RANK, BLOCK), shape(N_ROW, RANK + 16, BLOCK)],
        [SMEM, SMEM, VMEM, VMEM, VMEM],
        1_000_000_000,
        8 << 20,
        name="product",
    )(pairs, count, tiles, qr, qc)


def inverse_factor(gram):
    eye = (
        lax.broadcasted_iota(jnp.int32, (RANK, RANK), 0)
        == lax.broadcasted_iota(jnp.int32, (RANK, RANK), 1)
    ).astype(F32)
    work = jnp.concatenate([gram, eye], axis=1)
    row_id = lax.broadcasted_iota(jnp.int32, (RANK, 1), 0)
    for k in range(RANK):
        top = work[k : k + 1, :]
        factor = jnp.where(row_id > k, work[:, k : k + 1] / top[:, k : k + 1], 0.0)
        work = work - factor * top
    diagonal = jnp.sum(work[:, :RANK] * eye, axis=1, keepdims=True)
    return lax.rsqrt(diagonal) * work[:, RANK:]


def eps_eye():
    same = lax.broadcasted_iota(jnp.int32, (RANK, RANK), 0) == lax.broadcasted_iota(
        jnp.int32, (RANK, RANK), 1
    )
    return jnp.where(same, GRAM_EPS, 0.0).astype(F32)


def dot_t(a, b):
    return lax.dot_general(
        a, b, (((1,), (1,)), ((), ())), precision=HIGHEST, preferred_element_type=F32
    )


def mid2_body(rr_ref, cc_ref, p_ref, q_ref, gram_ref):
    total = total_of(rr_ref, cc_ref)
    packed = cc_ref[0, RANK:]
    for k in range(1, N_ROW):
        packed = packed + cc_ref[k, RANK:]
    gram = jnp.concatenate([packed[:, 64 * q : 64 * q + 64] for q in range(4)], axis=0)
    inverse = inverse_factor(gram / CELLS + eps_eye())
    normal = jnp.dot(inverse, total, precision=HIGHEST, preferred_element_type=F32)
    p_ref[...] = normal
    q_ref[...] = normal.astype(BF16)
    gram_ref[...] = dot_t(normal, normal)


def mid2(rr, cc):
    return call(
        mid2_body,
        [shape(RANK, BLOCK), shape(RANK, BLOCK, dtype=BF16), shape(RANK, RANK)],
        [VMEM, VMEM],
        10_000_000,
        2 << 20,
        name="mid2",
    )(rr, cc)


def project_body(pairs, count, tiles_ref, qr_ref, qc_ref, gram_ref, out_ref, cols_ref):
    cols_ref[...] = jnp.zeros_like(cols_ref)

    def one(slot, carry):
        i = pairs[2 * slot] % N_COL
        j = pairs[2 * slot + 1] // N_COL
        cols_ref[j] += jnp.dot(qr_ref[i], tiles_ref[slot], preferred_element_type=F32)
        return carry

    lax.fori_loop(0, count[0], one, 0)
    form = jnp.zeros((RANK, RANK), F32)
    for k in range(N_ROW):
        form = form + dot_t(cols_ref[k], qc_ref[k].astype(F32))
    out_ref[:, :RANK] = form
    out_ref[:, RANK:] = gram_ref[...]


def project(pairs, count, tiles, qr, qc, gram):
    return call(
        project_body,
        shape(RANK, 2 * RANK),
        [SMEM, SMEM, VMEM, VMEM, VMEM, VMEM],
        500_000_000,
        6 << 20,
        scratch=[pltpu.VMEM((N_ROW, RANK, BLOCK), F32)],
        name="project",
    )(pairs, count, tiles, qr, qc, gram)


def finish_body(parts_ref, p_ref, basis_ref, form_ref):
    total = parts_ref[0]
    for k in range(1, N_COL):
        total = total + parts_ref[k]
    inverse = inverse_factor(total[:, RANK:] / CELLS + eps_eye())
    basis_ref[...] = jnp.dot(inverse, p_ref[...], precision=HIGHEST, preferred_element_type=F32)
    half = total[:, :RANK] / CELLS
    right = dot_t(half, inverse)
    form = jnp.dot(inverse, right, precision=HIGHEST, preferred_element_type=F32)
    form_ref[...] = form + form.T


def finish(parts, p):
    return call(
        finish_body,
        [shape(RANK, BLOCK), shape(RANK, RANK)],
        [VMEM, VMEM],
        10_000_000,
        1 << 20,
        name="finish",
    )(parts, p)


def swap(x, axis):
    return lax.all_to_all(x, axis, 0, 0, tiled=True)


def spread(x, axis):
    size = lax.axis_size(axis)
    return swap(jnp.broadcast_to(x[None], (size,) + x.shape), axis)


def local(series, lag_weight, start_basis, block_pairs, pair_count):
    pairs = block_pairs.reshape(2 * SLOTS)
    count = pair_count.reshape(1)
    at = lax.all_gather(series.T, "col", axis=0)
    col_series = spread(series, "row")
    sums = day_sums(col_series)
    xr = spread(start_basis, "col")
    xc = spread(start_basis, "row")
    tiles, rows, cols = build(pairs, count, lag_weight, at, sums, xr, xc)
    q1 = mid1(swap(rows, "col"), swap(cols, "row"))
    rows, cols = product(pairs, count, tiles, spread(q1, "col"), spread(q1, "row"))
    p2, q2, gram = mid2(swap(rows, "col"), swap(cols, "row"))
    part = project(pairs, count, tiles, spread(q2, "col"), spread(q2, "row"), gram)
    part = jnp.sum(spread(part, "row"), axis=0)
    return finish(spread(part, "col"), p2)


def solution(mesh):
    return jax.shard_map(
        local,
        mesh=mesh,
        in_specs=(
            P(None, ("row", "col")),
            P(),
            P(None, ("row", "col")),
            P("row", "col", None, None),
            P("row", "col"),
        ),
        out_specs=(P(None, ("row", "col")), P()),
        check_vma=False,
    )
```

```python
import jax
import jax.numpy as jnp
from jax import lax
from jax.experimental import pallas as pl
from jax.experimental.pallas import tpu as pltpu
from jax.sharding import PartitionSpec as P

BLOCK = 256
DAYS = 512
LAGS = 4
RANK = 64
SLOTS = 32
N_ROW = 8
N_COL = 16
CELLS = 32768
BETA_CORR = 8.0
GRAM_EPS = 1e-05
TILE_SCALE = 0.25 / 16.0
HIGHEST = lax.Precision.HIGHEST
F32 = jnp.float32
BF16 = jnp.bfloat16
VMEM = pl.BlockSpec(memory_space=pltpu.VMEM)
ANY = pl.BlockSpec(memory_space=pl.ANY)
SMEM = pl.BlockSpec(memory_space=pltpu.SMEM)


def call(body, out_shape, in_specs, flops, nbytes, limit, scratch=(), name=None):
    many = isinstance(out_shape, (list, tuple))
    return pl.pallas_call(
        body,
        out_shape=out_shape,
        in_specs=in_specs,
        out_specs=[VMEM] * len(out_shape) if many else VMEM,
        scratch_shapes=list(scratch),
        compiler_params=pltpu.CompilerParams(vmem_limit_bytes=limit << 20),
        cost_estimate=pl.CostEstimate(flops=flops, bytes_accessed=nbytes, transcendentals=0),
        name=name,
    )


def shape(*dims, dtype=F32):
    return jax.ShapeDtypeStruct(dims, dtype)


def shift_body(own_ref, other_ref, out_ref, xc_ref):
    day = lax.broadcasted_iota(jnp.int32, (DAYS, BLOCK), 0)
    for core, ref in enumerate((own_ref, other_ref)):

        def one(step, carry, core=core, ref=ref):
            block = 4 * core + step
            x = ref[step, :DAYS].astype(F32)
            out_ref[block, 0] = (x + x).astype(BF16)
            for lag in range(1, LAGS):
                later = jnp.where(day < DAYS - lag, pltpu.roll(x, DAYS - lag, 0), 0.0)
                earlier = jnp.where(day >= lag, pltpu.roll(x, lag, 0), 0.0)
                out_ref[block, lag] = (later + earlier).astype(BF16)
            xc_ref[block] = ref[step, DAYS:]
            return carry

        lax.fori_loop(0, 4, one, 0)


def day_sums(own, other):
    return call(
        shift_body,
        [shape(N_ROW, LAGS, DAYS, BLOCK, dtype=BF16), shape(N_ROW, RANK, BLOCK, dtype=BF16)],
        [VMEM, VMEM],
        10_000_000,
        24 << 20,
        16,
        name="day_sums",
    )(own, other)


HALF = BLOCK // 2


def build_body(pairs, count, place, weight, sums_ref, xc_ref, *rest):
    first, second = rest[:4], rest[4:8]
    tiles_ref, rows_ref, cols_ref, at_ref, xr_ref, sems = rest[8:]
    copies = []

    def fetch(src, dst):
        copies.append(pltpu.make_async_copy(src, dst, sems.at[len(copies)]))
        copies[-1].start()

    for k in range(4):
        fetch(first[k].at[:, :HALF], at_ref.at[k, :, :HALF])
        fetch(second[k].at[:, :HALF], at_ref.at[:, k, HALF:])
        for q in range(2):
            lanes = slice(BLOCK * q, BLOCK * q + BLOCK)
            fetch(first[k].at[:, HALF:, lanes], xr_ref.at[k, :, 32 * q : 32 * q + 16])
            fetch(second[k].at[:, HALF:, lanes], xr_ref.at[:, k, 32 * q + 16 : 32 * q + 32])
    rows_ref[...] = jnp.zeros_like(rows_ref)
    cols_ref[...] = jnp.zeros_like(cols_ref)
    for copy in copies:
        copy.wait()

    def one(slot, carry):
        i = pairs[2 * slot] % N_COL
        j = pairs[2 * slot + 1] // N_COL
        from_y = (place[2] - i // 4) & 3
        from_z = (place[3] - i) & 3
        from_row = ((j ^ place[1]) & 1) * 4 + ((place[0] - j // 2) & 3)
        lead = at_ref[from_y, from_z]
        total = None
        for lag in range(LAGS):
            lagged = jnp.dot(lead, sums_ref[from_row, lag], preferred_element_type=F32)
            term = weight[lag] * jnp.tanh(lagged * (BETA_CORR / DAYS))
            total = term if total is None else total + term
        tile = (total * TILE_SCALE).astype(BF16)
        tiles_ref[slot] = tile
        cols_ref[j] += jnp.dot(xr_ref[from_y, from_z], tile, preferred_element_type=F32)
        rows_ref[i] += lax.dot_general(
            xc_ref[from_row], tile, (((1,), (1,)), ((), ())), preferred_element_type=F32
        )
        return carry

    lax.fori_loop(0, count[0], one, 0)


def build(pairs, count, place, weight, sums, xc, first, second):
    return call(
        build_body,
        [
            shape(SLOTS, BLOCK, BLOCK, dtype=BF16),
            shape(N_COL, RANK, BLOCK),
            shape(N_ROW, RANK, BLOCK),
        ],
        [SMEM] * 4 + [VMEM] * 2 + [ANY] * 8,
        9_000_000_000,
        20 << 20,
        28,
        scratch=[
            pltpu.VMEM((4, 4, BLOCK, DAYS), BF16),
            pltpu.VMEM((4, 4, RANK, BLOCK), BF16),
            pltpu.SemaphoreType.DMA((24,)),
        ],
        name="build",
    )(pairs, count, place, weight, sums, xc, *first, *second)


def total_of(rr_ref, cc_ref):
    total = rr_ref[0] + cc_ref[0, :RANK]
    for k in range(1, N_COL):
        total = total + rr_ref[k]
    for k in range(1, N_ROW):
        total = total + cc_ref[k, :RANK]
    return total


def mid1_body(rr_ref, cc_ref, out_ref):
    total = total_of(rr_ref, cc_ref)
    high = total.astype(BF16)
    out_ref[:RANK] = high
    out_ref[RANK:] = (total - high.astype(F32)).astype(BF16)


def mid1(rr, cc):
    return call(mid1_body, shape(2 * RANK, BLOCK, dtype=BF16), [VMEM, VMEM], 1_000_000, 2 << 20, 6, name="mid1")(rr, cc)


def product_body(pairs, count, tiles_ref, qr_ref, qc_ref, rows_ref, cols_ref):
    rows_ref[...] = jnp.zeros_like(rows_ref)
    cols_ref[...] = jnp.zeros_like(cols_ref)

    def one(slot, carry):
        i = pairs[2 * slot] % N_COL
        j = pairs[2 * slot + 1] // N_COL
        tile = tiles_ref[slot]
        into_cols = jnp.dot(qr_ref[i], tile, preferred_element_type=F32)
        into_rows = lax.dot_general(
            qc_ref[j], tile, (((1,), (1,)), ((), ())), preferred_element_type=F32
        )
        cols_ref[j, :RANK] += into_cols[:RANK] + into_cols[RANK:]
        rows_ref[i] += into_rows[:RANK] + into_rows[RANK:]
        return carry

    lax.fori_loop(0, count[0], one, 0)
    gram = jnp.zeros((RANK, RANK), F32)
    for k in range(N_COL):
        both = lax.dot_general(
            qr_ref[k, :RANK], qr_ref[k], (((1,), (1,)), ((), ())), preferred_element_type=F32
        )
        low_high = lax.dot_general(
            qr_ref[k, RANK:], qr_ref[k, :RANK], (((1,), (1,)), ((), ())), preferred_element_type=F32
        )
        gram = gram + both[:, :RANK] + (both[:, RANK:] + low_high)
    for k in range(N_ROW):
        for q in range(4):
            cols_ref[k, RANK:, 64 * q : 64 * q + 64] = gram[16 * q : 16 * q + 16]


def product(pairs, count, tiles, qr, qc):
    return call(
        product_body,
        [shape(N_COL, RANK, BLOCK), shape(N_ROW, RANK + 16, BLOCK)],
        [SMEM, SMEM, VMEM, VMEM, VMEM],
        1_000_000_000,
        8 << 20,
        16,
        name="product",
    )(pairs, count, tiles, qr, qc)


def inverse_factor(gram):
    eye = (
        lax.broadcasted_iota(jnp.int32, (RANK, RANK), 0)
        == lax.broadcasted_iota(jnp.int32, (RANK, RANK), 1)
    ).astype(F32)
    work = jnp.concatenate([gram, eye], axis=1)
    row_id = lax.broadcasted_iota(jnp.int32, (RANK, 1), 0)
    for k in range(RANK):
        top = work[k : k + 1, :]
        factor = jnp.where(row_id > k, work[:, k : k + 1] / top[:, k : k + 1], 0.0)
        work = work - factor * top
    diagonal = jnp.sum(work[:, :RANK] * eye, axis=1, keepdims=True)
    return lax.rsqrt(diagonal) * work[:, RANK:]


def eps_eye():
    same = lax.broadcasted_iota(jnp.int32, (RANK, RANK), 0) == lax.broadcasted_iota(
        jnp.int32, (RANK, RANK), 1
    )
    return jnp.where(same, GRAM_EPS, 0.0).astype(F32)


def dot_t(a, b):
    return lax.dot_general(
        a, b, (((1,), (1,)), ((), ())), precision=HIGHEST, preferred_element_type=F32
    )


def mid2_body(rr_ref, cc_ref, p_ref, q_ref, gram_ref):
    total = total_of(rr_ref, cc_ref)
    packed = cc_ref[0, RANK:]
    for k in range(1, N_ROW):
        packed = packed + cc_ref[k, RANK:]
    gram = jnp.concatenate([packed[:, 64 * q : 64 * q + 64] for q in range(4)], axis=0)
    inverse = inverse_factor(gram / CELLS + eps_eye())
    normal = jnp.dot(inverse, total, precision=HIGHEST, preferred_element_type=F32)
    p_ref[...] = normal
    q_ref[...] = normal.astype(BF16)
    gram_ref[...] = dot_t(normal, normal)


def mid2(rr, cc):
    return call(
        mid2_body,
        [shape(RANK, BLOCK), shape(RANK, BLOCK, dtype=BF16), shape(RANK, RANK)],
        [VMEM, VMEM],
        10_000_000,
        2 << 20,
        8,
        name="mid2",
    )(rr, cc)


def project_body(pairs, count, tiles_ref, qr_ref, qc_ref, gram_ref, out_ref, cols_ref):
    cols_ref[...] = jnp.zeros_like(cols_ref)

    def one(slot, carry):
        i = pairs[2 * slot] % N_COL
        j = pairs[2 * slot + 1] // N_COL
        cols_ref[j] += jnp.dot(qr_ref[i], tiles_ref[slot], preferred_element_type=F32)
        return carry

    lax.fori_loop(0, count[0], one, 0)
    form = jnp.zeros((RANK, RANK), F32)
    for k in range(N_ROW):
        form = form + dot_t(cols_ref[k], qc_ref[k].astype(F32))
    out_ref[:, :RANK] = form
    out_ref[:, RANK:] = gram_ref[...]


def project(pairs, count, tiles, qr, qc, gram):
    return call(
        project_body,
        shape(RANK, 2 * RANK),
        [SMEM, SMEM, VMEM, VMEM, VMEM, VMEM],
        500_000_000,
        6 << 20,
        12,
        scratch=[pltpu.VMEM((N_ROW, RANK, BLOCK), F32)],
        name="project",
    )(pairs, count, tiles, qr, qc, gram)


def finish_body(parts_ref, p_ref, basis_ref, form_ref):
    total = parts_ref[0]
    for k in range(1, N_COL):
        total = total + parts_ref[k]
    inverse = inverse_factor(total[:, RANK:] / CELLS + eps_eye())
    basis_ref[...] = jnp.dot(inverse, p_ref[...], precision=HIGHEST, preferred_element_type=F32)
    half = total[:, :RANK] / CELLS
    right = dot_t(half, inverse)
    form = jnp.dot(inverse, right, precision=HIGHEST, preferred_element_type=F32)
    form_ref[...] = form + form.T


def finish(parts, p):
    return call(
        finish_body,
        [shape(RANK, BLOCK), shape(RANK, RANK)],
        [VMEM, VMEM],
        10_000_000,
        1 << 20,
        6,
        name="finish",
    )(parts, p)


def swap(x, axis):
    return lax.all_to_all(x, axis, 0, 0, tiled=True)


def spread(x, axis):
    size = lax.axis_size(axis)
    return swap(jnp.broadcast_to(x[None], (size,) + x.shape), axis)


def shift(x, axis, k):
    if axis == "x":
        pairs = [(d, (d // 2 + k) % 4 * 2 + d % 2) for d in range(N_ROW)]
    elif axis == "core":
        pairs = [(d, d ^ k) for d in range(N_ROW)]
    elif axis == "y":
        pairs = [(d, (d // 4 + k) % 4 * 4 + d % 4) for d in range(N_COL)]
    else:
        pairs = [(d, d // 4 * 4 + (d + k) % 4) for d in range(N_COL)]
    return lax.ppermute(x, "row" if axis in ("x", "core") else "col", pairs)


def around(x, axis):
    return [x] + [shift(x, axis, k) for k in range(1, 4)]


def local(series, lag_weight, start_basis, block_pairs, pair_count):
    pairs = block_pairs.reshape(2 * SLOTS)
    count = pair_count.reshape(1)
    row, col = lax.axis_index("row"), lax.axis_index("col")
    place = jnp.stack([row // 2, row % 2, col // 4, col % 4]).astype(jnp.int32)
    lead = series.T
    packed = jnp.concatenate([start_basis[:32], start_basis[32:]], axis=1)
    first = around(jnp.concatenate([lead[:HALF], packed[:16]], axis=0), "z")
    second = around(jnp.concatenate([lead[HALF:], packed[16:]], axis=0), "y")
    trail = around(jnp.concatenate([series, start_basis], axis=0), "x")
    first, second, trail = lax.optimization_barrier((first, second, trail))
    first = around(jnp.stack(first), "y")
    second = around(jnp.stack(second), "z")
    own = jnp.stack(trail)
    sums, xc = day_sums(own, shift(own, "core", 1))
    tiles, rows, cols = build(pairs, count, place, lag_weight, sums, xc, first, second)
    q1 = mid1(swap(rows, "col"), swap(cols, "row"))
    rows, cols = product(pairs, count, tiles, spread(q1, "col"), spread(q1, "row"))
    p2, q2, gram = mid2(swap(rows, "col"), swap(cols, "row"))
    part = project(pairs, count, tiles, spread(q2, "col"), spread(q2, "row"), gram)
    part = jnp.sum(spread(part, "row"), axis=0)
    return finish(spread(part, "col"), p2)


def solution(mesh):
    return jax.shard_map(
        local,
        mesh=mesh,
        in_specs=(
            P(None, ("row", "col")),
            P(),
            P(None, ("row", "col")),
            P("row", "col", None, None),
            P("row", "col"),
        ),
        out_specs=(P(None, ("row", "col")), P()),
        check_vma=False,
    )
```

```python
import jax
import jax.numpy as jnp
from jax import lax
from jax.experimental import pallas as pl
from jax.experimental.pallas import tpu as pltpu
from jax.sharding import PartitionSpec as P

BLOCK = 256
DAYS = 512
LAGS = 4
RANK = 64
SLOTS = 32
N_ROW = 8
N_COL = 16
CELLS = 32768
BETA_CORR = 8.0
GRAM_EPS = 1e-05
TILE_SCALE = 0.25 / 16.0
HIGHEST = lax.Precision.HIGHEST
F32 = jnp.float32
BF16 = jnp.bfloat16
VMEM = pl.BlockSpec(memory_space=pltpu.VMEM)
ANY = pl.BlockSpec(memory_space=pl.ANY)
SMEM = pl.BlockSpec(memory_space=pltpu.SMEM)


def call(body, out_shape, in_specs, flops, nbytes, limit, scratch=(), name=None):
    many = isinstance(out_shape, (list, tuple))
    return pl.pallas_call(
        body,
        out_shape=out_shape,
        in_specs=in_specs,
        out_specs=[VMEM] * len(out_shape) if many else VMEM,
        scratch_shapes=list(scratch),
        compiler_params=pltpu.CompilerParams(vmem_limit_bytes=limit << 20),
        cost_estimate=pl.CostEstimate(flops=flops, bytes_accessed=nbytes, transcendentals=0),
        name=name,
    )


def shape(*dims, dtype=F32):
    return jax.ShapeDtypeStruct(dims, dtype)


def shift_body(own_ref, other_ref, out_ref, xc_ref):
    day = lax.broadcasted_iota(jnp.int32, (DAYS, BLOCK), 0)
    for core, ref in enumerate((own_ref, other_ref)):

        def one(step, carry, core=core, ref=ref):
            block = 4 * core + step
            x = ref[step, :DAYS].astype(F32)
            out_ref[block, 0] = (x + x).astype(BF16)
            for lag in range(1, LAGS):
                later = jnp.where(day < DAYS - lag, pltpu.roll(x, DAYS - lag, 0), 0.0)
                earlier = jnp.where(day >= lag, pltpu.roll(x, lag, 0), 0.0)
                out_ref[block, lag] = (later + earlier).astype(BF16)
            xc_ref[block] = ref[step, DAYS:]
            return carry

        lax.fori_loop(0, 4, one, 0)


def day_sums(own, other):
    return call(
        shift_body,
        [shape(N_ROW, LAGS, DAYS, BLOCK, dtype=BF16), shape(N_ROW, RANK, BLOCK, dtype=BF16)],
        [VMEM, VMEM],
        10_000_000,
        24 << 20,
        16,
        name="day_sums",
    )(own, other)


HALF = BLOCK // 2
GROUP = 4


def row_offset(place, j):
    return ((j ^ place[1]) & 1) * 4 + ((place[0] - j // 2) & 3)


def groups_of(count):
    return (count[0] + GROUP - 1) // GROUP


def build_body(pairs, count, place, weight, sums_ref, xc_ref, *rest):
    first, second = rest[:4], rest[4:8]
    tiles_ref, rows_ref, cols_ref, at_ref, xr_ref, last_ref, sems = rest[8:]
    copies = []

    def fetch(src, dst):
        copies.append(pltpu.make_async_copy(src, dst, sems.at[len(copies)]))
        copies[-1].start()

    for k in range(4):
        fetch(first[k].at[:, :HALF], at_ref.at[k, :, :HALF])
        fetch(second[k].at[:, :HALF], at_ref.at[:, k, HALF:])
        for q in range(2):
            lanes = slice(BLOCK * q, BLOCK * q + BLOCK)
            fetch(first[k].at[:, HALF:, lanes], xr_ref.at[k, :, 32 * q : 32 * q + 16])
            fetch(second[k].at[:, HALF:, lanes], xr_ref.at[:, k, 32 * q + 16 : 32 * q + 32])
    rows_ref[...] = jnp.zeros_like(rows_ref)
    cols_ref[...] = jnp.zeros_like(cols_ref)
    for copy in copies:
        copy.wait()

    def add_products(tile, i, from_y, from_z, from_row):
        cols_ref[from_row] += jnp.dot(xr_ref[from_y, from_z], tile, preferred_element_type=F32)
        rows_ref[i] += lax.dot_general(
            xc_ref[from_row], tile, (((1,), (1,)), ((), ())), preferred_element_type=F32
        )

    def indices(slot):
        i = pairs[2 * slot] % N_COL
        from_y = (place[2] - i // 4) & 3
        from_z = (place[3] - i) & 3
        return i, from_y, from_z, row_offset(place, pairs[2 * slot + 1] // N_COL)

    last_ref[...] = jnp.zeros_like(last_ref)

    def one(slot, carry):
        add_products(last_ref[...], *indices(jnp.maximum(slot - 1, 0)))
        i, from_y, from_z, from_row = indices(slot)
        lead = at_ref[from_y, from_z]
        total = None
        for lag in range(LAGS):
            lagged = jnp.dot(lead, sums_ref[from_row, lag], preferred_element_type=F32)
            term = weight[lag] * jnp.tanh(lagged * (BETA_CORR / DAYS))
            total = term if total is None else total + term
        tile = (total * TILE_SCALE).astype(BF16)
        tiles_ref[slot] = tile
        last_ref[...] = tile
        return carry

    lax.fori_loop(0, count[0], one, 0)
    add_products(last_ref[...], *indices(count[0] - 1))

    def clear(slot, carry):
        tiles_ref[slot] = jnp.zeros((BLOCK, BLOCK), BF16)
        return carry

    lax.fori_loop(count[0], groups_of(count) * GROUP, clear, 0)


def build(pairs, count, place, weight, sums, xc, first, second):
    return call(
        build_body,
        [
            shape(SLOTS, BLOCK, BLOCK, dtype=BF16),
            shape(N_COL, RANK, BLOCK),
            shape(N_ROW, RANK, BLOCK),
        ],
        [SMEM] * 4 + [VMEM] * 2 + [ANY] * 8,
        9_000_000_000,
        20 << 20,
        28,
        scratch=[
            pltpu.VMEM((4, 4, BLOCK, DAYS), BF16),
            pltpu.VMEM((4, 4, RANK, BLOCK), BF16),
            pltpu.VMEM((BLOCK, BLOCK), BF16),
            pltpu.SemaphoreType.DMA((24,)),
        ],
        name="build",
    )(pairs, count, place, weight, sums, xc, *first, *second)


def total_of(rr_ref, own_ref, parts):
    total = rr_ref[0] + own_ref[0, :RANK]
    for k in range(1, N_COL):
        total = total + rr_ref[k]
    for part in parts:
        total = total + part[0, :RANK]
    return total


def mid1_body(rr_ref, own_ref, a_ref, b_ref, c_ref, out_ref, wide_ref):
    total = total_of(rr_ref, own_ref, (a_ref, b_ref, c_ref))
    high = total.astype(BF16)
    both = jnp.concatenate([high, (total - high.astype(F32)).astype(BF16)], axis=0)
    out_ref[...] = both
    for k in range(N_COL):
        wide_ref[k] = both


def mid1(rr, own, parts):
    return call(
        mid1_body,
        [shape(2 * RANK, BLOCK, dtype=BF16), shape(N_COL, 2 * RANK, BLOCK, dtype=BF16)],
        [VMEM] * 5,
        1_000_000,
        4 << 20,
        8,
        name="mid1",
    )(rr, own, *parts)


def join(near_ref, far_ref, joined_ref):
    joined_ref[:4] = near_ref[...]
    joined_ref[4:] = far_ref[...]


def product_body(pairs, count, place, tiles_ref, qr_ref, near_ref, far_ref, rows_ref, cols_ref, qc_ref):
    rows_ref[...] = jnp.zeros_like(rows_ref)
    cols_ref[...] = jnp.zeros_like(cols_ref)
    join(near_ref, far_ref, qc_ref)

    def some(group, carry):
        done = []
        for k in range(GROUP):
            slot = group * GROUP + k
            i = pairs[2 * slot] % N_COL
            j = row_offset(place, pairs[2 * slot + 1] // N_COL)
            tile = tiles_ref[slot]
            into_cols = jnp.dot(qr_ref[i], tile, preferred_element_type=F32)
            into_rows = lax.dot_general(
                qc_ref[j], tile, (((1,), (1,)), ((), ())), preferred_element_type=F32
            )
            done.append((i, j, into_rows[:RANK] + into_rows[RANK:], into_cols[:RANK] + into_cols[RANK:]))
        for i, j, into_rows, into_cols in done:
            cols_ref[j, :RANK] += into_cols
            rows_ref[i] += into_rows
        return carry

    lax.fori_loop(0, groups_of(count), some, 0)
    gram = jnp.zeros((RANK, RANK), F32)
    for k in range(N_COL):
        both = lax.dot_general(
            qr_ref[k, :RANK], qr_ref[k], (((1,), (1,)), ((), ())), preferred_element_type=F32
        )
        low_high = lax.dot_general(
            qr_ref[k, RANK:], qr_ref[k, :RANK], (((1,), (1,)), ((), ())), preferred_element_type=F32
        )
        gram = gram + both[:, :RANK] + (both[:, RANK:] + low_high)
    for k in range(N_ROW):
        for q in range(4):
            cols_ref[k, RANK:, 64 * q : 64 * q + 64] = gram[16 * q : 16 * q + 16]


def product(pairs, count, place, tiles, qr, near, far):
    return call(
        product_body,
        [shape(N_COL, RANK, BLOCK), shape(N_ROW, RANK + 16, BLOCK)],
        [SMEM] * 3 + [VMEM] * 4,
        1_000_000_000,
        8 << 20,
        16,
        scratch=[pltpu.VMEM((N_ROW, 2 * RANK, BLOCK), BF16)],
        name="product",
    )(pairs, count, place, tiles, qr, near, far)


def inverse_factor(gram):
    eye = (
        lax.broadcasted_iota(jnp.int32, (RANK, RANK), 0)
        == lax.broadcasted_iota(jnp.int32, (RANK, RANK), 1)
    ).astype(F32)
    work = jnp.concatenate([gram, eye], axis=1)
    row_id = lax.broadcasted_iota(jnp.int32, (RANK, 1), 0)
    for k in range(RANK):
        top = work[k : k + 1, :]
        factor = jnp.where(row_id > k, work[:, k : k + 1] / top[:, k : k + 1], 0.0)
        work = work - factor * top
    diagonal = jnp.sum(work[:, :RANK] * eye, axis=1, keepdims=True)
    return lax.rsqrt(diagonal) * work[:, RANK:]


def eps_eye():
    same = lax.broadcasted_iota(jnp.int32, (RANK, RANK), 0) == lax.broadcasted_iota(
        jnp.int32, (RANK, RANK), 1
    )
    return jnp.where(same, GRAM_EPS, 0.0).astype(F32)


def dot_t(a, b):
    return lax.dot_general(
        a, b, (((1,), (1,)), ((), ())), precision=HIGHEST, preferred_element_type=F32
    )


def mid2_body(rr_ref, own_ref, a_ref, b_ref, c_ref, p_ref, q_ref, wide_ref, gram_ref):
    parts = (a_ref, b_ref, c_ref)
    total = total_of(rr_ref, own_ref, parts)
    packed = own_ref[0, RANK:]
    for part in parts:
        packed = packed + part[0, RANK:]
    gram = jnp.concatenate([packed[:, 64 * q : 64 * q + 64] for q in range(4)], axis=0)
    inverse = inverse_factor(gram / CELLS + eps_eye())
    normal = jnp.dot(inverse, total, precision=HIGHEST, preferred_element_type=F32)
    p_ref[...] = normal
    rounded = normal.astype(BF16)
    q_ref[...] = rounded
    for k in range(N_COL):
        wide_ref[k] = rounded
    gram_ref[...] = dot_t(normal, normal)


def mid2(rr, own, parts):
    return call(
        mid2_body,
        [
            shape(RANK, BLOCK),
            shape(RANK, BLOCK, dtype=BF16),
            shape(N_COL, RANK, BLOCK, dtype=BF16),
            shape(RANK, RANK),
        ],
        [VMEM] * 5,
        10_000_000,
        2 << 20,
        8,
        name="mid2",
    )(rr, own, *parts)


def project_body(
    pairs, count, place, tiles_ref, qr_ref, near_ref, far_ref, gram_ref, out_ref, cols_ref, qc_ref
):
    cols_ref[...] = jnp.zeros_like(cols_ref)
    join(near_ref, far_ref, qc_ref)

    def some(group, carry):
        done = []
        for k in range(GROUP):
            slot = group * GROUP + k
            i = pairs[2 * slot] % N_COL
            j = row_offset(place, pairs[2 * slot + 1] // N_COL)
            done.append((j, jnp.dot(qr_ref[i], tiles_ref[slot], preferred_element_type=F32)))
        for j, into_cols in done:
            cols_ref[j] += into_cols
        return carry

    lax.fori_loop(0, groups_of(count), some, 0)
    form = jnp.zeros((RANK, RANK), F32)
    for k in range(N_ROW):
        form = form + dot_t(cols_ref[k], qc_ref[k].astype(F32))
    both = jnp.concatenate([form, gram_ref[...]], axis=1)
    for k in range(N_ROW):
        out_ref[k] = both


def project(pairs, count, place, tiles, qr, near, far, gram):
    return call(
        project_body,
        shape(N_ROW, RANK, 2 * RANK),
        [SMEM] * 3 + [VMEM] * 5,
        500_000_000,
        6 << 20,
        12,
        scratch=[pltpu.VMEM((N_ROW, RANK, BLOCK), F32), pltpu.VMEM((N_ROW, RANK, BLOCK), BF16)],
        name="project",
    )(pairs, count, place, tiles, qr, near, far, gram)


def finish_body(parts_ref, p_ref, basis_ref, form_ref):
    total = parts_ref[0]
    for k in range(1, N_COL):
        total = total + parts_ref[k]
    inverse = inverse_factor(total[:, RANK:] / CELLS + eps_eye())
    basis_ref[...] = jnp.dot(inverse, p_ref[...], precision=HIGHEST, preferred_element_type=F32)
    half = total[:, :RANK] / CELLS
    right = dot_t(half, inverse)
    form = jnp.dot(inverse, right, precision=HIGHEST, preferred_element_type=F32)
    form_ref[...] = form + form.T


def finish(parts, p):
    return call(
        finish_body,
        [shape(RANK, BLOCK), shape(RANK, RANK)],
        [VMEM, VMEM],
        10_000_000,
        1 << 20,
        6,
        name="finish",
    )(parts, p)


def swap(x, axis):
    return lax.all_to_all(x, axis, 0, 0, tiled=True)


def spread(x, axis):
    size = lax.axis_size(axis)
    return swap(jnp.broadcast_to(x[None], (size,) + x.shape), axis)


def shift(x, axis, k):
    if axis == "x":
        pairs = [(d, (d // 2 + k) % 4 * 2 + d % 2) for d in range(N_ROW)]
    elif axis == "core":
        pairs = [(d, d ^ k) for d in range(N_ROW)]
    elif axis == "y":
        pairs = [(d, (d // 4 + k) % 4 * 4 + d % 4) for d in range(N_COL)]
    else:
        pairs = [(d, d // 4 * 4 + (d + k) % 4) for d in range(N_COL)]
    return lax.ppermute(x, "row" if axis in ("x", "core") else "col", pairs)


def around(x, axis):
    return [x] + [shift(x, axis, k) for k in range(1, 4)]


def scatter(rows, cols):
    own = cols[:4] + shift(cols[4:], "core", 1)
    parts = [shift(own[k : k + 1], "x", 4 - k) for k in range(1, 4)]
    return swap(rows, "col"), own, parts


def gather(q, wide):
    near = around(q, "x")
    qr = swap(wide, "col")
    near = jnp.stack(near)
    return qr, near, shift(near, "core", 1)


def local(series, lag_weight, start_basis, block_pairs, pair_count):
    pairs = block_pairs.reshape(2 * SLOTS)
    count = pair_count.reshape(1)
    row, col = lax.axis_index("row"), lax.axis_index("col")
    place = jnp.stack([row // 2, row % 2, col // 4, col % 4]).astype(jnp.int32)
    lead = series.T
    packed = jnp.concatenate([start_basis[:32], start_basis[32:]], axis=1)
    first = around(jnp.concatenate([lead[:HALF], packed[:16]], axis=0), "z")
    second = around(jnp.concatenate([lead[HALF:], packed[16:]], axis=0), "y")
    trail = around(jnp.concatenate([series, start_basis], axis=0), "x")
    first, second, trail = lax.optimization_barrier((first, second, trail))
    first = around(jnp.stack(first), "y")
    second = around(jnp.stack(second), "z")
    own = jnp.stack(trail)
    sums, xc = day_sums(own, shift(own, "core", 1))
    tiles, rows, cols = build(pairs, count, place, lag_weight, sums, xc, first, second)
    q1, wide = mid1(*scatter(rows, cols))
    rows, cols = product(pairs, count, place, tiles, *gather(q1, wide))
    p2, q2, wide, gram = mid2(*scatter(rows, cols))
    part = project(pairs, count, place, tiles, *gather(q2, wide), gram)
    part = jnp.sum(swap(part, "row"), axis=0)
    return finish(spread(part, "col"), p2)


def solution(mesh):
    return jax.shard_map(
        local,
        mesh=mesh,
        in_specs=(
            P(None, ("row", "col")),
            P(),
            P(None, ("row", "col")),
            P("row", "col", None, None),
            P("row", "col"),
        ),
        out_specs=(P(None, ("row", "col")), P()),
        check_vma=False,
    )
```

```python
import jax
import jax.numpy as jnp
from jax import lax
from jax.experimental import pallas as pl
from jax.experimental.pallas import tpu as pltpu
from jax.sharding import PartitionSpec as P


BLOCK = 256
DAYS = 512
LAGS = 4
RANK = 64
SLOTS = 32
N_ROW = 8
N_COL = 16
CELLS = 32768
BETA_CORR = 8.0
GRAM_EPS = 1e-05
TILE_SCALE = 0.25 / 16.0
HIGHEST = lax.Precision.HIGHEST
F32 = jnp.float32
BF16 = jnp.bfloat16
VMEM = pl.BlockSpec(memory_space=pltpu.VMEM)
HBM = pl.BlockSpec(memory_space=pltpu.HBM)
ANY = pl.BlockSpec(memory_space=pl.ANY)
SMEM = pl.BlockSpec(memory_space=pltpu.SMEM)


def call(body, out_shape, in_specs, flops, nbytes, limit, scratch=(), out_specs=None):
    many = isinstance(out_shape, (list, tuple))
    return pl.pallas_call(
        body,
        out_shape=out_shape,
        in_specs=in_specs,
        out_specs=out_specs or ([VMEM] * len(out_shape) if many else VMEM),
        scratch_shapes=list(scratch),
        compiler_params=pltpu.CompilerParams(vmem_limit_bytes=limit << 20),
        cost_estimate=pl.CostEstimate(flops=flops, bytes_accessed=nbytes, transcendentals=0),
    )


def shape(*dims, dtype=F32):
    return jax.ShapeDtypeStruct(dims, dtype)


def shift_body(own_ref, other_ref, out_ref, xc_ref):
    day = lax.broadcasted_iota(jnp.int32, (DAYS, BLOCK), 0)
    for core, ref in enumerate((own_ref, other_ref)):

        def one(step, carry, core=core, ref=ref):
            block = 4 * core + step
            x = ref[step, :DAYS].astype(F32) * (BETA_CORR / DAYS)
            out_ref[block, 0] = (x + x).astype(BF16)
            for lag in range(1, LAGS):
                later = jnp.where(day < DAYS - lag, pltpu.roll(x, DAYS - lag, 0), 0.0)
                earlier = jnp.where(day >= lag, pltpu.roll(x, lag, 0), 0.0)
                out_ref[block, lag] = (later + earlier).astype(BF16)
            xc_ref[block] = ref[step, DAYS:]
            return carry

        lax.fori_loop(0, 4, one, 0)


def day_sums(own, other):
    return call(
        shift_body,
        [shape(N_ROW, LAGS, DAYS, BLOCK, dtype=BF16), shape(N_ROW, RANK, BLOCK, dtype=BF16)],
        [VMEM, VMEM],
        10_000_000,
        24 << 20,
        16,
    )(own, other)


HALF = BLOCK // 2
GROUP = 4
TILE_ROOM = 288


def row_offset(place, j):
    return ((j ^ place[1]) & 1) * 4 + ((place[0] - j // 2) & 3)


def groups_of(count):
    return (count[0] + GROUP - 1) // GROUP


def build_body(pairs, count, place, weight, sums_ref, xc_ref, *rest):
    first, second = rest[:8], rest[8:16]
    tiles_ref, rows_ref, cols_ref, at_ref, xr_ref, buffer, sems, out_sems = rest[16:]
    copies = []

    def fetch(src, dst):
        copies.append(pltpu.make_async_copy(src, dst, sems.at[len(copies)]))
        copies[-1].start()

    for k in range(4):
        for h in range(2):
            two = slice(2 * h, 2 * h + 2)
            a, b = first[2 * k + h], second[2 * k + h]
            fetch(a.at[:, :HALF], at_ref.at[k, two, :HALF])
            fetch(b.at[:, :HALF], at_ref.at[two, k, HALF:])
            for q in range(2):
                lanes = slice(BLOCK * q, BLOCK * q + BLOCK)
                fetch(a.at[:, HALF:, lanes], xr_ref.at[k, two, 32 * q : 32 * q + 16])
                fetch(b.at[:, HALF:, lanes], xr_ref.at[two, k, 32 * q + 16 : 32 * q + 32])
    rows_ref[...] = jnp.zeros_like(rows_ref)
    cols_ref[...] = jnp.zeros_like(cols_ref)
    buffer[1] = jnp.zeros((2, BLOCK, BLOCK), BF16)
    for copy in copies:
        copy.wait()
    twos = (count[0] + 1) // 2

    def indices(slot):
        i = pairs[2 * slot] % N_COL
        from_y = (place[2] - i // 4) & 3
        from_z = (place[3] - i) & 3
        return i, from_y, from_z, row_offset(place, pairs[2 * slot + 1] // N_COL)

    def products(two, side):
        done = []
        for k in range(2):
            i, from_y, from_z, from_row = indices(2 * two + k)
            tile = buffer[side, k]
            into_cols = jnp.dot(xr_ref[from_y, from_z], tile, preferred_element_type=F32)
            into_rows = lax.dot_general(
                xc_ref[from_row], tile, (((1,), (1,)), ((), ())), preferred_element_type=F32
            )
            done.append((i, from_row, into_rows, into_cols))
        for i, from_row, into_rows, into_cols in done:
            cols_ref[from_row] += into_cols
            rows_ref[i] += into_rows

    def tile_of(slot):
        _, from_y, from_z, from_row = indices(slot)
        live = jnp.where(slot < count[0], TILE_SCALE, 0.0)
        lead = at_ref[from_y, from_z]
        total = None
        for lag in range(LAGS):
            lagged = jnp.dot(lead, sums_ref[from_row, lag], preferred_element_type=F32)
            term = weight[lag] * jnp.tanh(lagged)
            total = term if total is None else total + term
        return (total * live).astype(BF16)

    def store(two, side):
        return pltpu.make_async_copy(
            buffer.at[side], tiles_ref.at[pl.ds(2 * two, 2)], out_sems.at[side]
        )

    def one(two, carry):
        side = two & 1
        products(jnp.maximum(two - 1, 0), 1 - side)
        here, there = tile_of(2 * two), tile_of(2 * two + 1)

        @pl.when(two >= 2)
        def _():
            store(two - 2, side).wait()

        buffer[side, 0] = here
        buffer[side, 1] = there
        store(two, side).start()
        return carry

    lax.fori_loop(0, twos, one, 0)
    products(twos - 1, (twos - 1) & 1)

    @pl.when(twos >= 2)
    def _():
        store(twos - 2, twos & 1).wait()

    store(twos - 1, (twos - 1) & 1).wait()


def build(pairs, count, place, weight, sums, xc, first, second):
    return call(
        build_body,
        [
            shape(TILE_ROOM, BLOCK, BLOCK, dtype=BF16),
            shape(N_COL, RANK, BLOCK),
            shape(N_ROW, RANK, BLOCK),
        ],
        [SMEM] * 4 + [VMEM] * 2 + [ANY] * 16,
        9_000_000_000,
        20 << 20,
        30,
        scratch=[
            pltpu.VMEM((4, 4, BLOCK, DAYS), BF16),
            pltpu.VMEM((4, 4, RANK, BLOCK), BF16),
            pltpu.VMEM((2, 2, BLOCK, BLOCK), BF16),
            pltpu.SemaphoreType.DMA((48,)),
            pltpu.SemaphoreType.DMA((2,)),
        ],
        out_specs=[HBM, VMEM, VMEM],
    )(pairs, count, place, weight, sums, xc, *first, *second)


def total_of(rr_ref, own_ref, parts):
    total = rr_ref[0] + own_ref[0, :RANK]
    for k in range(1, N_COL):
        total = total + rr_ref[k]
    for part in parts:
        total = total + part[0, :RANK]
    return total


def mid1_body(rr_ref, own_ref, a_ref, b_ref, c_ref, out_ref, wide_ref):
    total = total_of(rr_ref, own_ref, (a_ref, b_ref, c_ref))
    high = total.astype(BF16)
    both = jnp.concatenate([high, (total - high.astype(F32)).astype(BF16)], axis=0)
    out_ref[...] = both
    for k in range(N_COL):
        wide_ref[k] = both


def mid1(rr, own, parts):
    return call(
        mid1_body,
        [shape(2 * RANK, BLOCK, dtype=BF16), shape(N_COL, 2 * RANK, BLOCK, dtype=BF16)],
        [VMEM] * 5,
        1_000_000,
        4 << 20,
        8,
    )(rr, own, *parts)


def load(tiles_ref, tiles, sems, group):
    slots = pl.ds(group * GROUP, GROUP)
    return pltpu.make_async_copy(tiles_ref.at[slots], tiles.at[slots], sems.at[group])


def load_all(count, tiles_ref, tiles, sems):
    def begin(group, carry):
        load(tiles_ref, tiles, sems, group).start()
        return carry

    lax.fori_loop(0, groups_of(count), begin, 0)


def arrive(count, tiles_ref, tiles, sems, group):
    load(tiles_ref, tiles, sems, group).wait()

    def clear(slot, carry):
        tiles[slot] = jnp.zeros((BLOCK, BLOCK), BF16)
        return carry

    lax.fori_loop(jnp.maximum(count[0], group * GROUP), group * GROUP + GROUP, clear, 0)


TILES = [pltpu.VMEM((SLOTS, BLOCK, BLOCK), BF16), pltpu.SemaphoreType.DMA((SLOTS // GROUP,))]


def join(near_ref, far_ref, joined_ref):
    joined_ref[:4] = near_ref[...]
    joined_ref[4:] = far_ref[...]


def product_body(pairs, count, place, tiles_ref, qr_ref, near_ref, far_ref, rows_ref, cols_ref, qc_ref, tiles, sems):
    load_all(count, tiles_ref, tiles, sems)
    rows_ref[...] = jnp.zeros_like(rows_ref)
    cols_ref[...] = jnp.zeros_like(cols_ref)
    join(near_ref, far_ref, qc_ref)

    def some(group, carry):
        arrive(count, tiles_ref, tiles, sems, group)
        done = []
        for k in range(GROUP):
            slot = group * GROUP + k
            i = pairs[2 * slot] % N_COL
            j = row_offset(place, pairs[2 * slot + 1] // N_COL)
            tile = tiles[slot]
            into_cols = jnp.dot(qr_ref[i], tile, preferred_element_type=F32)
            into_rows = lax.dot_general(
                qc_ref[j], tile, (((1,), (1,)), ((), ())), preferred_element_type=F32
            )
            done.append((i, j, into_rows[:RANK] + into_rows[RANK:], into_cols[:RANK] + into_cols[RANK:]))
        for i, j, into_rows, into_cols in done:
            cols_ref[j, :RANK] += into_cols
            rows_ref[i] += into_rows
        return carry

    lax.fori_loop(0, groups_of(count), some, 0)
    gram = jnp.zeros((RANK, RANK), F32)
    for k in range(N_COL):
        both = lax.dot_general(
            qr_ref[k, :RANK], qr_ref[k], (((1,), (1,)), ((), ())), preferred_element_type=F32
        )
        low_high = lax.dot_general(
            qr_ref[k, RANK:], qr_ref[k, :RANK], (((1,), (1,)), ((), ())), preferred_element_type=F32
        )
        gram = gram + both[:, :RANK] + (both[:, RANK:] + low_high)
    for k in range(N_ROW):
        for q in range(4):
            cols_ref[k, RANK:, 64 * q : 64 * q + 64] = gram[16 * q : 16 * q + 16]


def product(pairs, count, place, tiles, qr, near, far):
    return call(
        product_body,
        [shape(N_COL, RANK, BLOCK), shape(N_ROW, RANK + 16, BLOCK)],
        [SMEM] * 3 + [HBM] + [VMEM] * 3,
        1_000_000_000,
        8 << 20,
        30,
        scratch=[pltpu.VMEM((N_ROW, 2 * RANK, BLOCK), BF16)] + TILES,
    )(pairs, count, place, tiles, qr, near, far)


PANEL = 8
PACKED = RANK // 2 + 8


def inverse_factor(gram):
    eye = (
        lax.broadcasted_iota(jnp.int32, (RANK, RANK), 0)
        == lax.broadcasted_iota(jnp.int32, (RANK, RANK), 1)
    ).astype(F32)
    work = jnp.concatenate([gram, eye], axis=1)
    out = []
    for base in range(0, RANK, PANEL):
        rows = [work[p : p + 1, :] for p in range(PANEL)]
        entry = {
            (p, q): jnp.broadcast_to(rows[p][:, base + q : base + q + 1], (1, 2 * RANK))
            for p in range(PANEL)
            for q in range(p, PANEL)
        }
        work = work[PANEL:]
        more = base + PANEL < RANK
        factor = [
            jnp.broadcast_to(work[:, base + p : base + p + 1], work.shape)
            for p in range(PANEL if more else 0)
        ]
        for p in range(PANEL):
            inverse = 1.0 / entry[p, p]
            for q in range(p + 1, PANEL):
                ratio = entry[p, q] * inverse
                rows[q] = rows[q] - ratio * rows[p]
                for r in range(q, PANEL):
                    entry[q, r] = entry[q, r] - ratio * entry[p, r]
            if more:
                factor[p] = factor[p] * inverse
                for q in range(p + 1, PANEL):
                    factor[q] = factor[q] - factor[p] * entry[p, q]
            out.append(lax.rsqrt(entry[p, p]) * rows[p])
        if more:
            for p in range(PANEL):
                work = work - factor[p] * rows[p]
    return jnp.concatenate(out, axis=0)[:, RANK:]


def row_less_col(strict):
    row = lax.broadcasted_iota(jnp.int32, (RANK, RANK), 0)
    col = lax.broadcasted_iota(jnp.int32, (RANK, RANK), 1)
    return row < col if strict else row <= col


def eps_eye():
    same = lax.broadcasted_iota(jnp.int32, (RANK, RANK), 0) == lax.broadcasted_iota(
        jnp.int32, (RANK, RANK), 1
    )
    return jnp.where(same, GRAM_EPS, 0.0).astype(F32)


def dot_t(a, b):
    return lax.dot_general(
        a, b, (((1,), (1,)), ((), ())), precision=HIGHEST, preferred_element_type=F32
    )


def mid2_body(rr_ref, own_ref, a_ref, b_ref, c_ref, p_ref, q_ref, wide_ref, gram_ref):
    parts = (a_ref, b_ref, c_ref)
    total = total_of(rr_ref, own_ref, parts)
    packed = own_ref[0, RANK:]
    for part in parts:
        packed = packed + part[0, RANK:]
    gram = jnp.concatenate([packed[:, 64 * q : 64 * q + 64] for q in range(4)], axis=0)
    inverse = inverse_factor(gram / CELLS + eps_eye())
    normal = jnp.dot(inverse, total, precision=HIGHEST, preferred_element_type=F32)
    p_ref[...] = normal
    rounded = normal.astype(BF16)
    q_ref[...] = rounded
    for k in range(N_COL):
        wide_ref[k] = rounded
    gram_ref[...] = dot_t(normal, normal)


def mid2(rr, own, parts):
    return call(
        mid2_body,
        [
            shape(RANK, BLOCK),
            shape(RANK, BLOCK, dtype=BF16),
            shape(N_COL, RANK, BLOCK, dtype=BF16),
            shape(RANK, RANK),
        ],
        [VMEM] * 5,
        10_000_000,
        2 << 20,
        8,
    )(rr, own, *parts)


def project_body(
    pairs, count, place, tiles_ref, qr_ref, near_ref, far_ref, gram_ref, out_ref, cols_ref, qc_ref, tiles, sems
):
    load_all(count, tiles_ref, tiles, sems)
    cols_ref[...] = jnp.zeros_like(cols_ref)
    join(near_ref, far_ref, qc_ref)

    def some(group, carry):
        arrive(count, tiles_ref, tiles, sems, group)
        done = []
        for k in range(GROUP):
            slot = group * GROUP + k
            i = pairs[2 * slot] % N_COL
            j = row_offset(place, pairs[2 * slot + 1] // N_COL)
            done.append((j, jnp.dot(qr_ref[i], tiles[slot], preferred_element_type=F32)))
        for j, into_cols in done:
            cols_ref[j] += into_cols
        return carry

    lax.fori_loop(0, groups_of(count), some, 0)
    form = jnp.zeros((RANK, RANK), F32)
    for k in range(N_ROW):
        form = form + dot_t(cols_ref[k], qc_ref[k].astype(F32))
    gram = gram_ref[...]
    packed = jnp.where(row_less_col(False), form + form.T, gram)
    diagonal = jnp.sum(jnp.where(eps_eye() > 0.0, gram, 0.0), axis=0, keepdims=True)
    both = jnp.concatenate([packed[: RANK // 2], packed[RANK // 2 :]], axis=1)
    tail = jnp.concatenate([diagonal, jnp.zeros((1, RANK), F32)], axis=1)
    for k in range(N_ROW):
        out_ref[k, : RANK // 2] = both
        out_ref[k, RANK // 2 :] = jnp.broadcast_to(tail, (8, 2 * RANK))


def project(pairs, count, place, tiles, qr, near, far, gram):
    return call(
        project_body,
        shape(N_ROW, PACKED, 2 * RANK),
        [SMEM] * 3 + [HBM] + [VMEM] * 4,
        500_000_000,
        6 << 20,
        30,
        scratch=[pltpu.VMEM((N_ROW, RANK, BLOCK), F32), pltpu.VMEM((N_ROW, RANK, BLOCK), BF16)]
        + TILES,
    )(pairs, count, place, tiles, qr, near, far, gram)


def respread_body(parts_ref, out_ref):
    total = parts_ref[0]
    for k in range(1, N_ROW):
        total = total + parts_ref[k]
    for k in range(N_COL):
        out_ref[k] = total


def respread(parts):
    return call(respread_body, shape(N_COL, PACKED, 2 * RANK), [VMEM], 100_000, 1 << 19, 4)(parts)


def finish_body(parts_ref, p_ref, basis_ref, form_ref):
    total = parts_ref[0]
    for k in range(1, N_COL):
        total = total + parts_ref[k]
    top = total[: RANK // 2]
    packed = jnp.concatenate([top[:, :RANK], top[:, RANK:]], axis=0)
    lower = jnp.where(row_less_col(False), 0.0, packed)
    diagonal = jnp.where(eps_eye() > 0.0, total[RANK // 2 : RANK // 2 + 1, :RANK], 0.0)
    inverse = inverse_factor((lower + lower.T + diagonal) / CELLS + eps_eye())
    basis_ref[...] = jnp.dot(inverse, p_ref[...], precision=HIGHEST, preferred_element_type=F32)
    upper = jnp.where(row_less_col(False), packed, 0.0)
    form = (upper + jnp.where(row_less_col(True), packed, 0.0).T) / CELLS
    form_ref[...] = jnp.dot(
        inverse, dot_t(form, inverse), precision=HIGHEST, preferred_element_type=F32
    )


def finish(parts, p):
    return call(
        finish_body, [shape(RANK, BLOCK), shape(RANK, RANK)], [VMEM, VMEM], 10_000_000, 1 << 20, 6
    )(parts, p)


def swap(x, axis):
    return lax.all_to_all(x, axis, 0, 0, tiled=True)


def shift(x, axis, k):
    if axis == "x":
        pairs = [(d, (d // 2 + k) % 4 * 2 + d % 2) for d in range(N_ROW)]
    elif axis == "core":
        pairs = [(d, d ^ k) for d in range(N_ROW)]
    elif axis == "y":
        pairs = [(d, (d // 4 + k) % 4 * 4 + d % 4) for d in range(N_COL)]
    else:
        pairs = [(d, d // 4 * 4 + (d + k) % 4) for d in range(N_COL)]
    return lax.ppermute(x, "row" if axis in ("x", "core") else "col", pairs)


def around(x, axis):
    return [x] + [shift(x, axis, k) for k in range(1, 4)]


def both_ways(pieces, axis):
    low, high = jnp.stack(pieces[:2]), jnp.stack(pieces[2:])
    low_up, high_down = shift(low, axis, 1), shift(high, axis, 3)
    high_up, low_down = shift(high, axis, 1), shift(low, axis, 3)
    low_far, high_far = shift(low_up, axis, 1), shift(high_down, axis, 3)
    return [low, high, low_up, high_up, low_far, high_far, low_down, high_down]


def scatter(rows, cols):
    own = cols[:4] + shift(cols[4:], "core", 1)
    parts = [shift(own[k : k + 1], "x", 4 - k) for k in range(1, 4)]
    return swap(rows, "col"), own, parts


def gather(q, wide):
    near = around(q, "x")
    qr = swap(wide, "col")
    near = jnp.stack(near)
    return qr, near, shift(near, "core", 1)


def local(series, lag_weight, start_basis, block_pairs, pair_count):
    pairs = block_pairs.reshape(2 * SLOTS)
    count = pair_count.reshape(1)
    row, col = lax.axis_index("row"), lax.axis_index("col")
    place = jnp.stack([row // 2, row % 2, col // 4, col % 4]).astype(jnp.int32)
    lead = series.T
    packed = jnp.concatenate([start_basis[:32], start_basis[32:]], axis=1)
    first = jnp.concatenate([lead[:HALF], packed[:16]], axis=0)
    second = jnp.concatenate([lead[HALF:], packed[16:]], axis=0)
    trail = jnp.concatenate([series, start_basis], axis=0)
    first, second, trail = lax.optimization_barrier((first, second, trail))
    first, second = around(first, "z"), around(second, "y")
    trail = around(trail, "x")
    first, second = lax.optimization_barrier((first, second))
    first, second = both_ways(first, "y"), both_ways(second, "z")
    own = jnp.stack(trail)
    other = shift(own, "core", 1)
    sums, xc = day_sums(own, other)
    tiles, rows, cols = build(pairs, count, place, lag_weight, sums, xc, first, second)
    q1, wide = mid1(*scatter(rows, cols))
    rows, cols = product(pairs, count, place, tiles, *gather(q1, wide))
    p2, q2, wide, gram = mid2(*scatter(rows, cols))
    part = project(pairs, count, place, tiles, *gather(q2, wide), gram)
    return finish(swap(respread(swap(part, "row")), "col"), p2)


def solution(mesh):
    return jax.shard_map(
        local,
        mesh=mesh,
        in_specs=(
            P(None, ("row", "col")),
            P(),
            P(None, ("row", "col")),
            P("row", "col", None, None),
            P("row", "col"),
        ),
        out_specs=(P(None, ("row", "col")), P()),
        check_vma=False,
    )
```

```python
import jax
import jax.numpy as jnp
from jax import lax
from jax.experimental import pallas as pl
from jax.experimental.pallas import tpu as pltpu
from jax.sharding import PartitionSpec as P


BLOCK = 256
DAYS = 512
LAGS = 4
RANK = 64
SLOTS = 32
N_ROW = 8
N_COL = 16
CELLS = 32768
BETA_CORR = 8.0
GRAM_EPS = 1e-05
TILE_SCALE = 0.25 / 16.0
HIGHEST = lax.Precision.HIGHEST
F32 = jnp.float32
BF16 = jnp.bfloat16
VMEM = pl.BlockSpec(memory_space=pltpu.VMEM)
HBM = pl.BlockSpec(memory_space=pltpu.HBM)
ANY = pl.BlockSpec(memory_space=pl.ANY)
SMEM = pl.BlockSpec(memory_space=pltpu.SMEM)


def call(body, out_shape, in_specs, flops, nbytes, limit, scratch=(), out_specs=None):
    many = isinstance(out_shape, (list, tuple))
    return pl.pallas_call(
        body,
        out_shape=out_shape,
        in_specs=in_specs,
        out_specs=out_specs or ([VMEM] * len(out_shape) if many else VMEM),
        scratch_shapes=list(scratch),
        compiler_params=pltpu.CompilerParams(vmem_limit_bytes=limit << 20),
        cost_estimate=pl.CostEstimate(flops=flops, bytes_accessed=nbytes, transcendentals=0),
    )


def shape(*dims, dtype=F32):
    return jax.ShapeDtypeStruct(dims, dtype)


def shift_body(own_ref, other_ref, out_ref, xc_ref):
    day = lax.broadcasted_iota(jnp.int32, (DAYS, BLOCK), 0)
    for core, ref in enumerate((own_ref, other_ref)):

        def one(step, carry, core=core, ref=ref):
            block = 4 * core + step
            x = ref[step, :DAYS].astype(F32) * (BETA_CORR / DAYS)
            out_ref[block, 0] = (x + x).astype(BF16)
            for lag in range(1, LAGS):
                later = jnp.where(day < DAYS - lag, pltpu.roll(x, DAYS - lag, 0), 0.0)
                earlier = jnp.where(day >= lag, pltpu.roll(x, lag, 0), 0.0)
                out_ref[block, lag] = (later + earlier).astype(BF16)
            xc_ref[block] = ref[step, DAYS:]
            return carry

        lax.fori_loop(0, 4, one, 0)


def day_sums(own, other):
    return call(
        shift_body,
        [shape(N_ROW, LAGS, DAYS, BLOCK, dtype=BF16), shape(N_ROW, RANK, BLOCK, dtype=BF16)],
        [VMEM, VMEM],
        10_000_000,
        24 << 20,
        16,
    )(own, other)


HALF = BLOCK // 2
GROUP = 4
PLACE = 2 * SLOTS + 1
TILE_ROOM = 288


def count_of(table):
    return table[2 * SLOTS]


def row_offset(table, j):
    return ((j ^ table[PLACE + 1]) & 1) * 4 + ((table[PLACE] - j // 2) & 3)


def groups_of(table):
    return (count_of(table) + GROUP - 1) // GROUP


def build_body(table, weight, sums_ref, xc_ref, *rest):
    first, second = rest[:8], rest[8:16]
    tiles_ref, rows_ref, cols_ref, at_ref, xr_ref, buffer, sems, out_sems = rest[16:]
    copies = []

    def fetch(src, dst):
        copies.append(pltpu.make_async_copy(src, dst, sems.at[len(copies)]))
        copies[-1].start()

    for k in range(4):
        for h in range(2):
            two = slice(2 * h, 2 * h + 2)
            a, b = first[2 * k + h], second[2 * k + h]
            fetch(a.at[:, :HALF], at_ref.at[k, two, :HALF])
            fetch(b.at[:, :HALF], at_ref.at[two, k, HALF:])
            for q in range(2):
                lanes = slice(BLOCK * q, BLOCK * q + BLOCK)
                fetch(a.at[:, HALF:, lanes], xr_ref.at[k, two, 32 * q : 32 * q + 16])
                fetch(b.at[:, HALF:, lanes], xr_ref.at[two, k, 32 * q + 16 : 32 * q + 32])
    rows_ref[...] = jnp.zeros_like(rows_ref)
    cols_ref[...] = jnp.zeros_like(cols_ref)
    buffer[1] = jnp.zeros((GROUP, BLOCK, BLOCK), BF16)
    for copy in copies:
        copy.wait()
    groups = groups_of(table)

    def indices(slot):
        i = table[2 * slot] % N_COL
        from_y = (table[PLACE + 2] - i // 4) & 3
        from_z = (table[PLACE + 3] - i) & 3
        return i, from_y, from_z, row_offset(table, table[2 * slot + 1] // N_COL)

    def products(group, side):
        done = []
        for k in range(GROUP):
            i, from_y, from_z, from_row = indices(GROUP * group + k)
            tile = buffer[side, k]
            into_cols = jnp.dot(xr_ref[from_y, from_z], tile, preferred_element_type=F32)
            into_rows = lax.dot_general(
                xc_ref[from_row], tile, (((1,), (1,)), ((), ())), preferred_element_type=F32
            )
            done.append((i, from_row, into_rows, into_cols))
        for i, from_row, into_rows, into_cols in done:
            cols_ref[from_row] += into_cols
            rows_ref[i] += into_rows

    def tile_of(slot):
        _, from_y, from_z, from_row = indices(slot)
        live = jnp.where(slot < count_of(table), TILE_SCALE, 0.0)
        lead = at_ref[from_y, from_z]
        total = None
        for lag in range(LAGS):
            lagged = jnp.dot(lead, sums_ref[from_row, lag], preferred_element_type=F32)
            term = weight[lag] * jnp.tanh(lagged)
            total = term if total is None else total + term
        return (total * live).astype(BF16)

    def store(group, side):
        return pltpu.make_async_copy(
            buffer.at[side], tiles_ref.at[pl.ds(GROUP * group, GROUP)], out_sems.at[side]
        )

    def one(group, carry):
        side = group & 1
        products(jnp.maximum(group - 1, 0), 1 - side)
        made = [tile_of(GROUP * group + k) for k in range(GROUP)]

        @pl.when(group >= 2)
        def _():
            store(group - 2, side).wait()

        for k in range(GROUP):
            buffer[side, k] = made[k]
        store(group, side).start()
        return carry

    lax.fori_loop(0, groups, one, 0)
    products(groups - 1, (groups - 1) & 1)

    @pl.when(groups >= 2)
    def _():
        store(groups - 2, groups & 1).wait()

    store(groups - 1, (groups - 1) & 1).wait()


def build(table, weight, sums, xc, first, second):
    return call(
        build_body,
        [
            shape(TILE_ROOM, BLOCK, BLOCK, dtype=BF16),
            shape(N_COL, RANK, BLOCK),
            shape(N_ROW, RANK, BLOCK),
        ],
        [SMEM] * 2 + [VMEM] * 2 + [ANY] * 16,
        9_000_000_000,
        20 << 20,
        30,
        scratch=[
            pltpu.VMEM((4, 4, BLOCK, DAYS), BF16),
            pltpu.VMEM((4, 4, RANK, BLOCK), BF16),
            pltpu.VMEM((2, GROUP, BLOCK, BLOCK), BF16),
            pltpu.SemaphoreType.DMA((48,)),
            pltpu.SemaphoreType.DMA((2,)),
        ],
        out_specs=[HBM, VMEM, VMEM],
    )(table, weight, sums, xc, *first, *second)


def total_of(rr_ref, own_ref, parts):
    total = rr_ref[0] + own_ref[0, :RANK]
    for k in range(1, N_COL):
        total = total + rr_ref[k]
    for part in parts:
        total = total + part[0, :RANK]
    return total


def mid1_body(rr_ref, own_ref, a_ref, b_ref, c_ref, out_ref, wide_ref):
    total = total_of(rr_ref, own_ref, (a_ref, b_ref, c_ref))
    high = total.astype(BF16)
    both = jnp.concatenate([high, (total - high.astype(F32)).astype(BF16)], axis=0)
    out_ref[...] = both
    for k in range(N_COL):
        wide_ref[k] = both


def mid1(rr, own, parts):
    return call(
        mid1_body,
        [shape(2 * RANK, BLOCK, dtype=BF16), shape(N_COL, 2 * RANK, BLOCK, dtype=BF16)],
        [VMEM] * 5,
        1_000_000,
        4 << 20,
        8,
    )(rr, own, *parts)


def load(tiles_ref, tiles, sems, group):
    slots = pl.ds(group * GROUP, GROUP)
    return pltpu.make_async_copy(tiles_ref.at[slots], tiles.at[slots], sems.at[group])


def load_all(table, tiles_ref, tiles, sems):
    def begin(group, carry):
        load(tiles_ref, tiles, sems, group).start()
        return carry

    lax.fori_loop(0, groups_of(table), begin, 0)


TILES = [pltpu.VMEM((SLOTS, BLOCK, BLOCK), BF16), pltpu.SemaphoreType.DMA((SLOTS // GROUP,))]


def join(near_ref, far_ref, joined_ref):
    joined_ref[:4] = near_ref[...]
    joined_ref[4:] = far_ref[...]


def product_body(table, tiles_ref, qr_ref, near_ref, far_ref, rows_ref, cols_ref, qc_ref, tiles, sems):
    load_all(table, tiles_ref, tiles, sems)
    rows_ref[...] = jnp.zeros_like(rows_ref)
    cols_ref[...] = jnp.zeros_like(cols_ref)
    join(near_ref, far_ref, qc_ref)

    def some(group, carry):
        load(tiles_ref, tiles, sems, group).wait()
        done = []
        for k in range(GROUP):
            slot = group * GROUP + k
            i = table[2 * slot] % N_COL
            j = row_offset(table, table[2 * slot + 1] // N_COL)
            tile = tiles[slot]
            into_cols = jnp.dot(qr_ref[i], tile, preferred_element_type=F32)
            into_rows = lax.dot_general(
                qc_ref[j], tile, (((1,), (1,)), ((), ())), preferred_element_type=F32
            )
            done.append((i, j, into_rows[:RANK] + into_rows[RANK:], into_cols[:RANK] + into_cols[RANK:]))
        for i, j, into_rows, into_cols in done:
            cols_ref[j, :RANK] += into_cols
            rows_ref[i] += into_rows
        return carry

    lax.fori_loop(0, groups_of(table), some, 0)
    gram = jnp.zeros((RANK, RANK), F32)
    for k in range(N_COL):
        both = lax.dot_general(
            qr_ref[k, :RANK], qr_ref[k], (((1,), (1,)), ((), ())), preferred_element_type=F32
        )
        low_high = lax.dot_general(
            qr_ref[k, RANK:], qr_ref[k, :RANK], (((1,), (1,)), ((), ())), preferred_element_type=F32
        )
        gram = gram + both[:, :RANK] + (both[:, RANK:] + low_high)
    for k in range(N_ROW):
        for q in range(4):
            cols_ref[k, RANK:, 64 * q : 64 * q + 64] = gram[16 * q : 16 * q + 16]


def product(table, tiles, qr, near, far):
    return call(
        product_body,
        [shape(N_COL, RANK, BLOCK), shape(N_ROW, RANK + 16, BLOCK)],
        [SMEM] + [HBM] + [VMEM] * 3,
        1_000_000_000,
        8 << 20,
        30,
        scratch=[pltpu.VMEM((N_ROW, 2 * RANK, BLOCK), BF16)] + TILES,
    )(table, tiles, qr, near, far)


PANEL = 8
PACKED = RANK // 2 + 8


def inverse_factor(gram):
    eye = (
        lax.broadcasted_iota(jnp.int32, (RANK, RANK), 0)
        == lax.broadcasted_iota(jnp.int32, (RANK, RANK), 1)
    ).astype(F32)
    work = jnp.concatenate([gram, eye], axis=1)
    out = []
    for base in range(0, RANK, PANEL):
        rows = [work[p : p + 1, :] for p in range(PANEL)]
        entry = {
            (p, q): jnp.broadcast_to(rows[p][:, base + q : base + q + 1], (1, 2 * RANK))
            for p in range(PANEL)
            for q in range(p, PANEL)
        }
        work = work[PANEL:]
        more = base + PANEL < RANK
        factor = [
            jnp.broadcast_to(work[:, base + p : base + p + 1], work.shape)
            for p in range(PANEL if more else 0)
        ]
        for p in range(PANEL):
            inverse = 1.0 / entry[p, p]
            for q in range(p + 1, PANEL):
                ratio = entry[p, q] * inverse
                rows[q] = rows[q] - ratio * rows[p]
                for r in range(q, PANEL):
                    entry[q, r] = entry[q, r] - ratio * entry[p, r]
            if more:
                factor[p] = factor[p] * inverse
                for q in range(p + 1, PANEL):
                    factor[q] = factor[q] - factor[p] * entry[p, q]
            out.append(lax.rsqrt(entry[p, p]) * rows[p])
        if more:
            for p in range(PANEL):
                work = work - factor[p] * rows[p]
    return jnp.concatenate(out, axis=0)[:, RANK:]


def row_less_col(strict):
    row = lax.broadcasted_iota(jnp.int32, (RANK, RANK), 0)
    col = lax.broadcasted_iota(jnp.int32, (RANK, RANK), 1)
    return row < col if strict else row <= col


def eps_eye():
    same = lax.broadcasted_iota(jnp.int32, (RANK, RANK), 0) == lax.broadcasted_iota(
        jnp.int32, (RANK, RANK), 1
    )
    return jnp.where(same, GRAM_EPS, 0.0).astype(F32)


def dot_t(a, b):
    return lax.dot_general(
        a, b, (((1,), (1,)), ((), ())), precision=HIGHEST, preferred_element_type=F32
    )


def mid2_body(rr_ref, own_ref, a_ref, b_ref, c_ref, p_ref, q_ref, wide_ref, gram_ref):
    parts = (a_ref, b_ref, c_ref)
    total = total_of(rr_ref, own_ref, parts)
    packed = own_ref[0, RANK:]
    for part in parts:
        packed = packed + part[0, RANK:]
    gram = jnp.concatenate([packed[:, 64 * q : 64 * q + 64] for q in range(4)], axis=0)
    inverse = inverse_factor(gram / CELLS + eps_eye())
    normal = jnp.dot(inverse, total, precision=HIGHEST, preferred_element_type=F32)
    p_ref[...] = normal
    rounded = normal.astype(BF16)
    q_ref[...] = rounded
    for k in range(N_COL):
        wide_ref[k] = rounded
    gram_ref[...] = dot_t(normal, normal)


def mid2(rr, own, parts):
    return call(
        mid2_body,
        [
            shape(RANK, BLOCK),
            shape(RANK, BLOCK, dtype=BF16),
            shape(N_COL, RANK, BLOCK, dtype=BF16),
            shape(RANK, RANK),
        ],
        [VMEM] * 5,
        10_000_000,
        2 << 20,
        8,
    )(rr, own, *parts)


def project_body(
    table, tiles_ref, qr_ref, near_ref, far_ref, gram_ref, out_ref, cols_ref, qc_ref, tiles, sems
):
    load_all(table, tiles_ref, tiles, sems)
    cols_ref[...] = jnp.zeros_like(cols_ref)
    join(near_ref, far_ref, qc_ref)

    def some(group, carry):
        load(tiles_ref, tiles, sems, group).wait()
        done = []
        for k in range(GROUP):
            slot = group * GROUP + k
            i = table[2 * slot] % N_COL
            j = row_offset(table, table[2 * slot + 1] // N_COL)
            done.append((j, jnp.dot(qr_ref[i], tiles[slot], preferred_element_type=F32)))
        for j, into_cols in done:
            cols_ref[j] += into_cols
        return carry

    lax.fori_loop(0, groups_of(table), some, 0)
    form = jnp.zeros((RANK, RANK), F32)
    for k in range(N_ROW):
        high = cols_ref[k].astype(BF16)
        low = (cols_ref[k] - high.astype(F32)).astype(BF16)
        both = lax.dot_general(
            jnp.concatenate([high, low], axis=0),
            qc_ref[k],
            (((1,), (1,)), ((), ())),
            preferred_element_type=F32,
        )
        form = form + (both[:RANK] + both[RANK:])
    gram = gram_ref[...]
    packed = jnp.where(row_less_col(False), form + form.T, gram)
    diagonal = jnp.sum(jnp.where(eps_eye() > 0.0, gram, 0.0), axis=0, keepdims=True)
    both = jnp.concatenate([packed[: RANK // 2], packed[RANK // 2 :]], axis=1)
    tail = jnp.concatenate([diagonal, jnp.zeros((1, RANK), F32)], axis=1)
    out_ref[: RANK // 2] = both
    out_ref[RANK // 2 :] = jnp.broadcast_to(tail, (8, 2 * RANK))


def project(table, tiles, qr, near, far, gram):
    return call(
        project_body,
        shape(PACKED, 2 * RANK),
        [SMEM] + [HBM] + [VMEM] * 4,
        500_000_000,
        6 << 20,
        30,
        scratch=[pltpu.VMEM((N_ROW, RANK, BLOCK), F32), pltpu.VMEM((N_ROW, RANK, BLOCK), BF16)]
        + TILES,
    )(table, tiles, qr, near, far, gram)


def finish_body(own_ref, a_ref, b_ref, c_ref, p_ref, basis_ref, form_ref):
    total = sum_of_four(own_ref[...], a_ref[...], b_ref[...], c_ref[...])
    top = total[: RANK // 2]
    packed = jnp.concatenate([top[:, :RANK], top[:, RANK:]], axis=0)
    lower = jnp.where(row_less_col(False), 0.0, packed)
    diagonal = jnp.where(eps_eye() > 0.0, total[RANK // 2 : RANK // 2 + 1, :RANK], 0.0)
    inverse = inverse_factor((lower + lower.T + diagonal) / CELLS + eps_eye())
    basis_ref[...] = jnp.dot(inverse, p_ref[...], precision=HIGHEST, preferred_element_type=F32)
    upper = jnp.where(row_less_col(False), packed, 0.0)
    form = (upper + jnp.where(row_less_col(True), packed, 0.0).T) / CELLS
    form_ref[...] = jnp.dot(
        inverse, dot_t(form, inverse), precision=HIGHEST, preferred_element_type=F32
    )


def sum_of_four(own, one, two, three):
    return (own + two) + (one + three)


def finish(parts, p):
    return call(
        finish_body, [shape(RANK, BLOCK), shape(RANK, RANK)], [VMEM] * 5, 10_000_000, 1 << 20, 6
    )(*parts, p)


def swap(x, axis):
    return lax.all_to_all(x, axis, 0, 0, tiled=True)


def shift(x, axis, k):
    if axis == "x":
        pairs = [(d, (d // 2 + k) % 4 * 2 + d % 2) for d in range(N_ROW)]
    elif axis == "core":
        pairs = [(d, d ^ k) for d in range(N_ROW)]
    elif axis == "y":
        pairs = [(d, (d // 4 + k) % 4 * 4 + d % 4) for d in range(N_COL)]
    else:
        pairs = [(d, d // 4 * 4 + (d + k) % 4) for d in range(N_COL)]
    return lax.ppermute(x, "row" if axis in ("x", "core") else "col", pairs)


def around(x, axis):
    return [x] + [shift(x, axis, k) for k in range(1, 4)]


def both_ways(pieces, axis):
    low, high = jnp.stack(pieces[:2]), jnp.stack(pieces[2:])
    low_up, high_down = shift(low, axis, 1), shift(high, axis, 3)
    high_up, low_down = shift(high, axis, 1), shift(low, axis, 3)
    low_far, high_far = shift(low_up, axis, 1), shift(high_down, axis, 3)
    return [low, high, low_up, high_up, low_far, high_far, low_down, high_down]


def scatter(rows, cols):
    own = cols[:4] + shift(cols[4:], "core", 1)
    parts = [shift(own[k : k + 1], "x", 4 - k) for k in range(1, 4)]
    return swap(rows, "col"), own, parts


def gather(q, wide):
    near = around(q, "x")
    qr = swap(wide, "col")
    near = jnp.stack(near)
    return qr, near, shift(near, "core", 1)


def local(series, lag_weight, start_basis, block_pairs, pair_count):
    row, col = lax.axis_index("row"), lax.axis_index("col")
    place = jnp.stack([row // 2, row % 2, col // 4, col % 4]).astype(jnp.int32)
    table = jnp.concatenate([block_pairs.reshape(2 * SLOTS), pair_count.reshape(1), place])
    lead = series.T
    packed = jnp.concatenate([start_basis[:32], start_basis[32:]], axis=1)
    first = jnp.concatenate([lead[:HALF], packed[:16]], axis=0)
    second = jnp.concatenate([lead[HALF:], packed[16:]], axis=0)
    trail = jnp.concatenate([series, start_basis], axis=0)
    first, second, trail = lax.optimization_barrier((first, second, trail))
    first, second = around(first, "z"), around(second, "y")
    trail = around(trail, "x")
    first, second = lax.optimization_barrier((first, second))
    first, second = both_ways(first, "y"), both_ways(second, "z")
    own = jnp.stack(trail)
    other = shift(own, "core", 1)
    sums, xc = day_sums(own, other)
    tiles, rows, cols = build(table, lag_weight, sums, xc, first, second)
    q1, wide = mid1(*scatter(rows, cols))
    rows, cols = product(table, tiles, *gather(q1, wide))
    p2, q2, wide, gram = mid2(*scatter(rows, cols))
    part = project(table, tiles, *gather(q2, wide), gram)
    part = part + shift(part, "core", 1)
    part = sum_of_four(*around(part, "x"))
    part = sum_of_four(*around(part, "z"))
    return finish(around(part, "y"), p2)


def solution(mesh):
    return jax.shard_map(
        local,
        mesh=mesh,
        in_specs=(
            P(None, ("row", "col")),
            P(),
            P(None, ("row", "col")),
            P("row", "col", None, None),
            P("row", "col"),
        ),
        out_specs=(P(None, ("row", "col")), P()),
        check_vma=False,
    )
```

```python
import jax
import jax.numpy as jnp
from jax import lax
from jax.experimental import pallas as pl
from jax.experimental.pallas import tpu as pltpu
from jax.sharding import PartitionSpec as P


BLOCK = 256
DAYS = 512
LAGS = 4
RANK = 64
SLOTS = 32
N_ROW = 8
N_COL = 16
CELLS = 32768
BETA_CORR = 8.0
GRAM_EPS = 1e-05
TILE_SCALE = 0.25 / 16.0
HIGHEST = lax.Precision.HIGHEST
F32 = jnp.float32
BF16 = jnp.bfloat16
VMEM = pl.BlockSpec(memory_space=pltpu.VMEM)
HBM = pl.BlockSpec(memory_space=pltpu.HBM)
ANY = pl.BlockSpec(memory_space=pl.ANY)
SMEM = pl.BlockSpec(memory_space=pltpu.SMEM)


def call(body, out_shape, in_specs, flops, nbytes, limit, scratch=(), out_specs=None):
    many = isinstance(out_shape, (list, tuple))
    return pl.pallas_call(
        body,
        out_shape=out_shape,
        in_specs=in_specs,
        out_specs=out_specs or ([VMEM] * len(out_shape) if many else VMEM),
        scratch_shapes=list(scratch),
        compiler_params=pltpu.CompilerParams(vmem_limit_bytes=limit << 20),
        cost_estimate=pl.CostEstimate(flops=flops, bytes_accessed=nbytes, transcendentals=0),
    )


def shape(*dims, dtype=F32):
    return jax.ShapeDtypeStruct(dims, dtype)


def shift_body(own_ref, other_ref, out_ref, xc_ref):
    day = lax.broadcasted_iota(jnp.int32, (DAYS, BLOCK), 0)
    for core, ref in enumerate((own_ref, other_ref)):

        def one(step, carry, core=core, ref=ref):
            block = 4 * core + step
            x = ref[step, :DAYS].astype(F32) * (BETA_CORR / DAYS)
            out_ref[block, 0] = (x + x).astype(BF16)
            for lag in range(1, LAGS):
                later = jnp.where(day < DAYS - lag, pltpu.roll(x, DAYS - lag, 0), 0.0)
                earlier = jnp.where(day >= lag, pltpu.roll(x, lag, 0), 0.0)
                out_ref[block, lag] = (later + earlier).astype(BF16)
            xc_ref[block] = ref[step, DAYS:]
            return carry

        lax.fori_loop(0, 4, one, 0)


def day_sums(own, other):
    return call(
        shift_body,
        [shape(N_ROW, LAGS, DAYS, BLOCK, dtype=BF16), shape(N_ROW, RANK, BLOCK, dtype=BF16)],
        [VMEM, VMEM],
        10_000_000,
        24 << 20,
        16,
    )(own, other)


HALF = BLOCK // 2
GROUP = 4
PLACE = 2 * SLOTS + 1
TILE_ROOM = 288


def count_of(table):
    return table[2 * SLOTS]


def row_offset(table, j):
    return ((j ^ table[PLACE + 1]) & 1) * 4 + ((table[PLACE] - j // 2) & 3)


def groups_of(table):
    return (count_of(table) + GROUP - 1) // GROUP


def build_body(table, weight, sums_ref, xc_ref, *rest):
    first, second = rest[:8], rest[8:16]
    tiles_ref, rows_ref, cols_ref, at_ref, buffer, sems, out_sems = rest[16:]
    copies = []

    def fetch(src, dst):
        copies.append(pltpu.make_async_copy(src, dst, sems.at[len(copies)]))
        copies[-1].start()

    for k in range(4):
        for h in range(2):
            two = slice(2 * h, 2 * h + 2)
            a, b = first[2 * k + h], second[2 * k + h]
            fetch(a, at_ref.at[k, two, : HALF + 16])
            fetch(b, at_ref.at[two, k, HALF + 16 :])
    rows_ref[...] = jnp.zeros_like(rows_ref)
    cols_ref[...] = jnp.zeros_like(cols_ref)
    buffer[1] = jnp.zeros((GROUP, BLOCK, BLOCK), BF16)
    for copy in copies:
        copy.wait()
    groups = groups_of(table)

    def indices(slot):
        i = table[2 * slot] % N_COL
        from_y = (table[PLACE + 2] - i // 4) & 3
        from_z = (table[PLACE + 3] - i) & 3
        return i, from_y, from_z, row_offset(table, table[2 * slot + 1] // N_COL)

    def basis_of(from_y, from_z):
        ends = [at_ref[from_y, from_z, :16], at_ref[from_y, from_z, 16 + BLOCK :]]
        return jnp.concatenate([e[:, BLOCK * q : BLOCK * q + BLOCK] for q in range(2) for e in ends], axis=0)

    def products(group, side):
        done = []
        for k in range(GROUP):
            i, from_y, from_z, from_row = indices(GROUP * group + k)
            tile = buffer[side, k]
            into_cols = jnp.dot(basis_of(from_y, from_z), tile, preferred_element_type=F32)
            into_rows = lax.dot_general(
                xc_ref[from_row], tile, (((1,), (1,)), ((), ())), preferred_element_type=F32
            )
            done.append((i, from_row, into_rows, into_cols))
        for i, from_row, into_rows, into_cols in done:
            cols_ref[from_row] += into_cols
            rows_ref[i] += into_rows

    def tile_of(slot):
        _, from_y, from_z, from_row = indices(slot)
        live = jnp.where(slot < count_of(table), TILE_SCALE, 0.0)
        lead = at_ref[from_y, from_z, 16 : 16 + BLOCK]
        total = None
        for lag in range(LAGS):
            lagged = jnp.dot(lead, sums_ref[from_row, lag], preferred_element_type=F32)
            term = weight[lag] * jnp.tanh(lagged)
            total = term if total is None else total + term
        return (total * live).astype(BF16)

    def store(group, side):
        return pltpu.make_async_copy(
            buffer.at[side], tiles_ref.at[pl.ds(GROUP * group, GROUP)], out_sems.at[side]
        )

    def one(group, carry):
        side = group & 1
        products(jnp.maximum(group - 1, 0), 1 - side)
        made = [tile_of(GROUP * group + k) for k in range(GROUP)]

        @pl.when(group >= 2)
        def _():
            store(group - 2, side).wait()

        for k in range(GROUP):
            buffer[side, k] = made[k]
        store(group, side).start()
        return carry

    lax.fori_loop(0, groups, one, 0)
    products(groups - 1, (groups - 1) & 1)

    @pl.when(groups >= 2)
    def _():
        store(groups - 2, groups & 1).wait()

    store(groups - 1, (groups - 1) & 1).wait()


def build(table, weight, sums, xc, first, second):
    return call(
        build_body,
        [
            shape(TILE_ROOM, BLOCK, BLOCK, dtype=BF16),
            shape(N_COL, RANK, BLOCK),
            shape(N_ROW, RANK, BLOCK),
        ],
        [SMEM] * 2 + [VMEM] * 2 + [ANY] * 16,
        9_000_000_000,
        20 << 20,
        30,
        scratch=[
            pltpu.VMEM((4, 4, BLOCK + 32, DAYS), BF16),
            pltpu.VMEM((2, GROUP, BLOCK, BLOCK), BF16),
            pltpu.SemaphoreType.DMA((16,)),
            pltpu.SemaphoreType.DMA((2,)),
        ],
        out_specs=[HBM, VMEM, VMEM],
    )(table, weight, sums, xc, *first, *second)


def total_of(rr_ref, own_ref, parts):
    total = rr_ref[0] + own_ref[0, :RANK]
    for k in range(1, N_COL):
        total = total + rr_ref[k]
    for part in parts:
        total = total + part[0, :RANK]
    return total


def mid1_body(rr_ref, own_ref, a_ref, b_ref, c_ref, out_ref, wide_ref):
    total = total_of(rr_ref, own_ref, (a_ref, b_ref, c_ref))
    high = total.astype(BF16)
    both = jnp.concatenate([high, (total - high.astype(F32)).astype(BF16)], axis=0)
    out_ref[...] = both
    for k in range(N_COL):
        wide_ref[k] = both


def mid1(rr, own, parts):
    return call(
        mid1_body,
        [shape(2 * RANK, BLOCK, dtype=BF16), shape(N_COL, 2 * RANK, BLOCK, dtype=BF16)],
        [VMEM] * 5,
        1_000_000,
        4 << 20,
        8,
    )(rr, own, *parts)


def load(tiles_ref, tiles, sems, group):
    slots = pl.ds(group * GROUP, GROUP)
    return pltpu.make_async_copy(tiles_ref.at[slots], tiles.at[slots], sems.at[group])


def load_all(table, tiles_ref, tiles, sems):
    def begin(group, carry):
        load(tiles_ref, tiles, sems, group).start()
        return carry

    lax.fori_loop(0, groups_of(table), begin, 0)


TILES = [pltpu.VMEM((SLOTS, BLOCK, BLOCK), BF16), pltpu.SemaphoreType.DMA((SLOTS // GROUP,))]


def join(near_ref, far_ref, joined_ref):
    joined_ref[:4] = near_ref[...]
    joined_ref[4:] = far_ref[...]


def product_body(table, tiles_ref, qr_ref, near_ref, far_ref, rows_ref, cols_ref, qc_ref, tiles, sems):
    load_all(table, tiles_ref, tiles, sems)
    rows_ref[...] = jnp.zeros_like(rows_ref)
    cols_ref[...] = jnp.zeros_like(cols_ref)
    join(near_ref, far_ref, qc_ref)
    gram = jnp.zeros((2 * RANK, 2 * RANK), F32)
    for k in range(N_COL):
        gram = gram + lax.dot_general(
            qr_ref[k], qr_ref[k], (((1,), (1,)), ((), ())), preferred_element_type=F32
        )
    gram = gram[:RANK, :RANK] + ((gram[:RANK, RANK:] + gram[RANK:, :RANK]) + gram[RANK:, RANK:])
    for k in range(N_ROW):
        for q in range(4):
            cols_ref[k, RANK:, 64 * q : 64 * q + 64] = gram[16 * q : 16 * q + 16]

    def some(group, carry):
        load(tiles_ref, tiles, sems, group).wait()
        done = []
        for k in range(GROUP):
            slot = group * GROUP + k
            i = table[2 * slot] % N_COL
            j = row_offset(table, table[2 * slot + 1] // N_COL)
            tile = tiles[slot]
            into_cols = jnp.dot(qr_ref[i], tile, preferred_element_type=F32)
            into_rows = lax.dot_general(
                qc_ref[j], tile, (((1,), (1,)), ((), ())), preferred_element_type=F32
            )
            done.append((i, j, into_rows[:RANK] + into_rows[RANK:], into_cols[:RANK] + into_cols[RANK:]))
        for i, j, into_rows, into_cols in done:
            cols_ref[j, :RANK] += into_cols
            rows_ref[i] += into_rows
        return carry

    lax.fori_loop(0, groups_of(table), some, 0)


def product(table, tiles, qr, near, far):
    return call(
        product_body,
        [shape(N_COL, RANK, BLOCK), shape(N_ROW, RANK + 16, BLOCK)],
        [SMEM] + [HBM] + [VMEM] * 3,
        1_000_000_000,
        8 << 20,
        30,
        scratch=[pltpu.VMEM((N_ROW, 2 * RANK, BLOCK), BF16)] + TILES,
    )(table, tiles, qr, near, far)


PANEL = 8
PACKED = RANK // 2 + 8


def inverse_factor(gram):
    eye = (
        lax.broadcasted_iota(jnp.int32, (RANK, RANK), 0)
        == lax.broadcasted_iota(jnp.int32, (RANK, RANK), 1)
    ).astype(F32)
    work = jnp.concatenate([gram, eye], axis=1)
    out = []
    for base in range(0, RANK, PANEL):
        rows = [work[p : p + 1, :] for p in range(PANEL)]
        entry = {
            (p, q): jnp.broadcast_to(rows[p][:, base + q : base + q + 1], (1, 2 * RANK))
            for p in range(PANEL)
            for q in range(p, PANEL)
        }
        work = work[PANEL:]
        more = base + PANEL < RANK
        factor = [
            jnp.broadcast_to(work[:, base + p : base + p + 1], work.shape)
            for p in range(PANEL if more else 0)
        ]
        for p in range(PANEL):
            inverse = 1.0 / entry[p, p]
            for q in range(p + 1, PANEL):
                ratio = entry[p, q] * inverse
                rows[q] = rows[q] - ratio * rows[p]
                for r in range(q, PANEL):
                    entry[q, r] = entry[q, r] - ratio * entry[p, r]
            if more:
                factor[p] = factor[p] * inverse
                for q in range(p + 1, PANEL):
                    factor[q] = factor[q] - factor[p] * entry[p, q]
            out.append(lax.rsqrt(entry[p, p]) * rows[p])
        if more:
            for p in range(PANEL):
                work = work - factor[p] * rows[p]
    return jnp.concatenate(out, axis=0)[:, RANK:]


def row_less_col(strict):
    row = lax.broadcasted_iota(jnp.int32, (RANK, RANK), 0)
    col = lax.broadcasted_iota(jnp.int32, (RANK, RANK), 1)
    return row < col if strict else row <= col


def eps_eye():
    same = lax.broadcasted_iota(jnp.int32, (RANK, RANK), 0) == lax.broadcasted_iota(
        jnp.int32, (RANK, RANK), 1
    )
    return jnp.where(same, GRAM_EPS, 0.0).astype(F32)


def dot_t(a, b):
    return lax.dot_general(
        a, b, (((1,), (1,)), ((), ())), precision=HIGHEST, preferred_element_type=F32
    )


def mid2_body(rr_ref, own_ref, a_ref, b_ref, c_ref, p_ref, q_ref, wide_ref, gram_ref):
    parts = (a_ref, b_ref, c_ref)
    total = total_of(rr_ref, own_ref, parts)
    packed = own_ref[0, RANK:]
    for part in parts:
        packed = packed + part[0, RANK:]
    gram = jnp.concatenate([packed[:, 64 * q : 64 * q + 64] for q in range(4)], axis=0)
    inverse = inverse_factor(gram / CELLS + eps_eye())
    normal = jnp.dot(inverse, total, precision=HIGHEST, preferred_element_type=F32)
    p_ref[...] = normal
    rounded = normal.astype(BF16)
    q_ref[...] = rounded
    for k in range(N_COL):
        wide_ref[k] = rounded
    gram_ref[...] = dot_t(normal, normal)


def mid2(rr, own, parts):
    return call(
        mid2_body,
        [
            shape(RANK, BLOCK),
            shape(RANK, BLOCK, dtype=BF16),
            shape(N_COL, RANK, BLOCK, dtype=BF16),
            shape(RANK, RANK),
        ],
        [VMEM] * 5,
        10_000_000,
        2 << 20,
        8,
    )(rr, own, *parts)


def project_body(
    table, tiles_ref, qr_ref, near_ref, far_ref, gram_ref, out_ref, cols_ref, qc_ref, tiles, sems
):
    load_all(table, tiles_ref, tiles, sems)
    cols_ref[...] = jnp.zeros_like(cols_ref)
    join(near_ref, far_ref, qc_ref)

    def some(group, carry):
        load(tiles_ref, tiles, sems, group).wait()
        done = []
        for k in range(GROUP):
            slot = group * GROUP + k
            i = table[2 * slot] % N_COL
            j = row_offset(table, table[2 * slot + 1] // N_COL)
            done.append((j, jnp.dot(qr_ref[i], tiles[slot], preferred_element_type=F32)))
        for j, into_cols in done:
            cols_ref[j] += into_cols
        return carry

    lax.fori_loop(0, groups_of(table), some, 0)
    form = jnp.zeros((RANK, RANK), F32)
    for k in range(N_ROW):
        high = cols_ref[k].astype(BF16)
        low = (cols_ref[k] - high.astype(F32)).astype(BF16)
        both = lax.dot_general(
            jnp.concatenate([high, low], axis=0),
            qc_ref[k],
            (((1,), (1,)), ((), ())),
            preferred_element_type=F32,
        )
        form = form + (both[:RANK] + both[RANK:])
    gram = gram_ref[...]
    packed = jnp.where(row_less_col(False), form + form.T, gram)
    diagonal = jnp.sum(jnp.where(eps_eye() > 0.0, gram, 0.0), axis=0, keepdims=True)
    both = jnp.concatenate([packed[: RANK // 2], packed[RANK // 2 :]], axis=1)
    tail = jnp.concatenate([diagonal, jnp.zeros((1, RANK), F32)], axis=1)
    out_ref[: RANK // 2] = both
    out_ref[RANK // 2 :] = jnp.broadcast_to(tail, (8, 2 * RANK))


def project(table, tiles, qr, near, far, gram):
    return call(
        project_body,
        shape(PACKED, 2 * RANK),
        [SMEM] + [HBM] + [VMEM] * 4,
        500_000_000,
        6 << 20,
        30,
        scratch=[pltpu.VMEM((N_ROW, RANK, BLOCK), F32), pltpu.VMEM((N_ROW, RANK, BLOCK), BF16)]
        + TILES,
    )(table, tiles, qr, near, far, gram)


def finish_body(own_ref, a_ref, b_ref, c_ref, p_ref, basis_ref, form_ref):
    total = sum_of_four(own_ref[...], a_ref[...], b_ref[...], c_ref[...])
    top = total[: RANK // 2]
    packed = jnp.concatenate([top[:, :RANK], top[:, RANK:]], axis=0)
    lower = jnp.where(row_less_col(False), 0.0, packed)
    diagonal = jnp.where(eps_eye() > 0.0, total[RANK // 2 : RANK // 2 + 1, :RANK], 0.0)
    inverse = inverse_factor((lower + lower.T + diagonal) / CELLS + eps_eye())
    basis_ref[...] = jnp.dot(inverse, p_ref[...], precision=HIGHEST, preferred_element_type=F32)
    upper = jnp.where(row_less_col(False), packed, 0.0)
    form = (upper + jnp.where(row_less_col(True), packed, 0.0).T) / CELLS
    form_ref[...] = jnp.dot(
        inverse, dot_t(form, inverse), precision=HIGHEST, preferred_element_type=F32
    )


def sum_of_four(own, one, two, three):
    return (own + two) + (one + three)


def finish(parts, p):
    return call(
        finish_body, [shape(RANK, BLOCK), shape(RANK, RANK)], [VMEM] * 5, 10_000_000, 1 << 20, 6
    )(*parts, p)


def swap(x, axis):
    return lax.all_to_all(x, axis, 0, 0, tiled=True)


def shift(x, axis, k):
    if axis == "x":
        pairs = [(d, (d // 2 + k) % 4 * 2 + d % 2) for d in range(N_ROW)]
    elif axis == "core":
        pairs = [(d, d ^ k) for d in range(N_ROW)]
    elif axis == "y":
        pairs = [(d, (d // 4 + k) % 4 * 4 + d % 4) for d in range(N_COL)]
    else:
        pairs = [(d, d // 4 * 4 + (d + k) % 4) for d in range(N_COL)]
    return lax.ppermute(x, "row" if axis in ("x", "core") else "col", pairs)


def around(x, axis):
    return [x] + [shift(x, axis, k) for k in range(1, 4)]


def both_ways(pieces, axis):
    low, high = jnp.stack(pieces[:2]), jnp.stack(pieces[2:])
    low_up, high_down = shift(low, axis, 1), shift(high, axis, 3)
    high_up, low_down = shift(high, axis, 1), shift(low, axis, 3)
    low_far, high_far = shift(low_up, axis, 1), shift(high_down, axis, 3)
    return [low, high, low_up, high_up, low_far, high_far, low_down, high_down]


def scatter(rows, cols):
    own = cols[:4] + shift(cols[4:], "core", 1)
    parts = [shift(own[k : k + 1], "x", 4 - k) for k in range(1, 4)]
    return swap(rows, "col"), own, parts


def gather(q, wide):
    near = around(q, "x")
    qr = swap(wide, "col")
    near = jnp.stack(near)
    return qr, near, shift(near, "core", 1)


def local(series, lag_weight, start_basis, block_pairs, pair_count):
    row, col = lax.axis_index("row"), lax.axis_index("col")
    place = jnp.stack([row // 2, row % 2, col // 4, col % 4]).astype(jnp.int32)
    table = jnp.concatenate([block_pairs.reshape(2 * SLOTS), pair_count.reshape(1), place])
    lead = series.T
    packed = jnp.concatenate([start_basis[:32], start_basis[32:]], axis=1)
    first = jnp.concatenate([packed[:16], lead[:HALF]], axis=0)
    second = jnp.concatenate([lead[HALF:], packed[16:]], axis=0)
    trail = jnp.concatenate([series, start_basis], axis=0)
    first, second, trail = lax.optimization_barrier((first, second, trail))
    first, second = around(first, "z"), around(second, "y")
    trail = around(trail, "x")
    first, second = both_ways(first, "y"), both_ways(second, "z")
    own = jnp.stack(trail)
    other = shift(own, "core", 1)
    sums, xc = day_sums(own, other)
    tiles, rows, cols = build(table, lag_weight, sums, xc, first, second)
    q1, wide = mid1(*scatter(rows, cols))
    rows, cols = product(table, tiles, *gather(q1, wide))
    p2, q2, wide, gram = mid2(*scatter(rows, cols))
    part = project(table, tiles, *gather(q2, wide), gram)
    part = part + shift(part, "core", 1)
    part = sum_of_four(*around(part, "x"))
    part = sum_of_four(*around(part, "z"))
    return finish(around(part, "y"), p2)


def solution(mesh):
    return jax.shard_map(
        local,
        mesh=mesh,
        in_specs=(
            P(None, ("row", "col")),
            P(),
            P(None, ("row", "col")),
            P("row", "col", None, None),
            P("row", "col"),
        ),
        out_specs=(P(None, ("row", "col")), P()),
        check_vma=False,
    )
```

```python
import jax
import jax.numpy as jnp
from jax import lax
from jax.experimental import pallas as pl
from jax.experimental.pallas import tpu as pltpu
from jax.sharding import PartitionSpec as P


BLOCK = 256
DAYS = 512
LAGS = 4
RANK = 64
SLOTS = 32
N_ROW = 8
N_COL = 16
CELLS = 32768
BETA_CORR = 8.0
GRAM_EPS = 1e-05
TILE_SCALE = 0.25 / 16.0
HIGHEST = lax.Precision.HIGHEST
F32 = jnp.float32
BF16 = jnp.bfloat16
VMEM = pl.BlockSpec(memory_space=pltpu.VMEM)
HBM = pl.BlockSpec(memory_space=pltpu.HBM)
ANY = pl.BlockSpec(memory_space=pl.ANY)
SMEM = pl.BlockSpec(memory_space=pltpu.SMEM)


def call(body, out_shape, in_specs, flops, nbytes, limit, scratch=(), out_specs=None):
    many = isinstance(out_shape, (list, tuple))
    return pl.pallas_call(
        body,
        out_shape=out_shape,
        in_specs=in_specs,
        out_specs=out_specs or ([VMEM] * len(out_shape) if many else VMEM),
        scratch_shapes=list(scratch),
        compiler_params=pltpu.CompilerParams(vmem_limit_bytes=limit << 20),
        cost_estimate=pl.CostEstimate(flops=flops, bytes_accessed=nbytes, transcendentals=0),
    )


def shape(*dims, dtype=F32):
    return jax.ShapeDtypeStruct(dims, dtype)


def pack_body(series_ref, start_ref, first_ref, second_ref, trail_ref):
    trail_ref[:DAYS] = series_ref[...]
    trail_ref[DAYS:] = start_ref[...]
    first_ref[:16, :BLOCK] = start_ref[:16]
    first_ref[:16, BLOCK:] = start_ref[32:48]
    second_ref[BLOCK // 2 :, :BLOCK] = start_ref[16:32]
    second_ref[BLOCK // 2 :, BLOCK:] = start_ref[48:]
    first_ref[16:] = series_ref[:, : BLOCK // 2].T
    second_ref[: BLOCK // 2] = series_ref[:, BLOCK // 2 :].T


def pack(series, start):
    half = shape(BLOCK // 2 + 16, DAYS, dtype=BF16)
    return call(
        pack_body,
        [half, half, shape(DAYS + RANK, BLOCK, dtype=BF16)],
        [VMEM, VMEM],
        100_000,
        1 << 20,
        4,
    )(series, start)


def shift_body(own_ref, other_ref, out_ref, xc_ref):
    day = lax.broadcasted_iota(jnp.int32, (DAYS, BLOCK), 0)
    for core, ref in enumerate((own_ref, other_ref)):

        def one(step, carry, core=core, ref=ref):
            block = 4 * core + step
            x = ref[step, :DAYS].astype(F32) * (BETA_CORR / DAYS)
            out_ref[block, 0] = (x + x).astype(BF16)
            for lag in range(1, LAGS):
                later = jnp.where(day < DAYS - lag, pltpu.roll(x, DAYS - lag, 0), 0.0)
                earlier = jnp.where(day >= lag, pltpu.roll(x, lag, 0), 0.0)
                out_ref[block, lag] = (later + earlier).astype(BF16)
            xc_ref[block] = ref[step, DAYS:]
            return carry

        lax.fori_loop(0, 4, one, 0)


def day_sums(own, other):
    return call(
        shift_body,
        [shape(N_ROW, LAGS, DAYS, BLOCK, dtype=BF16), shape(N_ROW, RANK, BLOCK, dtype=BF16)],
        [VMEM, VMEM],
        10_000_000,
        24 << 20,
        16,
    )(own, other)


HALF = BLOCK // 2
GROUP = 4
TILE_ROOM = 288


def count_of(table):
    return table[1][0, 0]


def row_offset(table, j):
    place = table[2]
    return ((j ^ place[1]) & 1) * 4 + ((place[0] - j // 2) & 3)


def groups_of(table):
    return (count_of(table) + GROUP - 1) // GROUP


def build_body(pairs, count, place, weight, sums_ref, xc_ref, *rest):
    table = (pairs, count, place)
    first, second = rest[:8], rest[8:16]
    tiles_ref, rows_ref, cols_ref, at_ref, buffer, sems, out_sems = rest[16:]
    copies = []

    def fetch(src, dst):
        copies.append(pltpu.make_async_copy(src, dst, sems.at[len(copies)]))
        copies[-1].start()

    for k in range(4):
        for h in range(2):
            two = slice(2 * h, 2 * h + 2)
            a, b = first[2 * k + h], second[2 * k + h]
            fetch(a, at_ref.at[k, two, : HALF + 16])
            fetch(b, at_ref.at[two, k, HALF + 16 :])
    rows_ref[...] = jnp.zeros_like(rows_ref)
    cols_ref[...] = jnp.zeros_like(cols_ref)
    buffer[1] = jnp.zeros((GROUP, BLOCK, BLOCK), BF16)
    for copy in copies:
        copy.wait()
    groups = groups_of(table)

    def indices(slot):
        i = table[0][0, slot] % N_COL
        from_y = (table[2][2] - i // 4) & 3
        from_z = (table[2][3] - i) & 3
        return i, from_y, from_z, row_offset(table, table[0][1, slot] // N_COL)

    def basis_of(from_y, from_z):
        ends = [at_ref[from_y, from_z, :16], at_ref[from_y, from_z, 16 + BLOCK :]]
        return jnp.concatenate([e[:, BLOCK * q : BLOCK * q + BLOCK] for q in range(2) for e in ends], axis=0)

    def products(group, side):
        done = []
        for k in range(GROUP):
            i, from_y, from_z, from_row = indices(GROUP * group + k)
            tile = buffer[side, k]
            into_cols = jnp.dot(basis_of(from_y, from_z), tile, preferred_element_type=F32)
            into_rows = lax.dot_general(
                xc_ref[from_row], tile, (((1,), (1,)), ((), ())), preferred_element_type=F32
            )
            done.append((i, from_row, into_rows, into_cols))
        for i, from_row, into_rows, into_cols in done:
            cols_ref[from_row] += into_cols
            rows_ref[i] += into_rows

    def tile_of(slot):
        _, from_y, from_z, from_row = indices(slot)
        live = jnp.where(slot < count_of(table), TILE_SCALE, 0.0)
        lead = at_ref[from_y, from_z, 16 : 16 + BLOCK]
        total = None
        for lag in range(LAGS):
            lagged = jnp.dot(lead, sums_ref[from_row, lag], preferred_element_type=F32)
            term = weight[lag] * jnp.tanh(lagged)
            total = term if total is None else total + term
        return (total * live).astype(BF16)

    def store(group, side):
        return pltpu.make_async_copy(
            buffer.at[side], tiles_ref.at[pl.ds(GROUP * group, GROUP)], out_sems.at[side]
        )

    def one(group, carry):
        side = group & 1
        products(jnp.maximum(group - 1, 0), 1 - side)
        made = [tile_of(GROUP * group + k) for k in range(GROUP)]

        @pl.when(group >= 2)
        def _():
            store(group - 2, side).wait()

        for k in range(GROUP):
            buffer[side, k] = made[k]
        store(group, side).start()
        return carry

    lax.fori_loop(0, groups, one, 0)
    products(groups - 1, (groups - 1) & 1)

    @pl.when(groups >= 2)
    def _():
        store(groups - 2, groups & 1).wait()

    store(groups - 1, (groups - 1) & 1).wait()


def build(table, weight, sums, xc, first, second):
    return call(
        build_body,
        [
            shape(TILE_ROOM, BLOCK, BLOCK, dtype=BF16),
            shape(N_COL, RANK, BLOCK),
            shape(N_ROW, RANK, BLOCK),
        ],
        [SMEM] * 4 + [VMEM] * 2 + [ANY] * 16,
        9_000_000_000,
        20 << 20,
        30,
        scratch=[
            pltpu.VMEM((4, 4, BLOCK + 32, DAYS), BF16),
            pltpu.VMEM((2, GROUP, BLOCK, BLOCK), BF16),
            pltpu.SemaphoreType.DMA((16,)),
            pltpu.SemaphoreType.DMA((2,)),
        ],
        out_specs=[HBM, VMEM, VMEM],
    )(*table, weight, sums, xc, *first, *second)


def total_of(rr_ref, own_ref, parts):
    total = rr_ref[0] + own_ref[0, :RANK]
    for k in range(1, N_COL):
        total = total + rr_ref[k]
    for part in parts:
        total = total + part[0, :RANK]
    return total


def mid1_body(rr_ref, own_ref, a_ref, b_ref, c_ref, out_ref, wide_ref):
    total = total_of(rr_ref, own_ref, (a_ref, b_ref, c_ref))
    high = total.astype(BF16)
    both = jnp.concatenate([high, (total - high.astype(F32)).astype(BF16)], axis=0)
    out_ref[...] = both
    for k in range(N_COL):
        wide_ref[k] = both


def mid1(rr, own, parts):
    return call(
        mid1_body,
        [shape(2 * RANK, BLOCK, dtype=BF16), shape(N_COL, 2 * RANK, BLOCK, dtype=BF16)],
        [VMEM] * 5,
        1_000_000,
        4 << 20,
        8,
    )(rr, own, *parts)


def load(tiles_ref, tiles, sems, group):
    slots = pl.ds(group * GROUP, GROUP)
    return pltpu.make_async_copy(tiles_ref.at[slots], tiles.at[slots], sems.at[group])


def load_all(table, tiles_ref, tiles, sems):
    def begin(group, carry):
        load(tiles_ref, tiles, sems, group).start()
        return carry

    lax.fori_loop(0, groups_of(table), begin, 0)


TILES = [pltpu.VMEM((SLOTS, BLOCK, BLOCK), BF16), pltpu.SemaphoreType.DMA((SLOTS // GROUP,))]


def join(near_ref, far_ref, joined_ref):
    joined_ref[:4] = near_ref[...]
    joined_ref[4:] = far_ref[...]


def product_body(
    pairs, count, place, tiles_ref, qr_ref, near_ref, far_ref, rows_ref, cols_ref, qc_ref, tiles, sems
):
    table = (pairs, count, place)
    load_all(table, tiles_ref, tiles, sems)
    rows_ref[...] = jnp.zeros_like(rows_ref)
    cols_ref[...] = jnp.zeros_like(cols_ref)
    join(near_ref, far_ref, qc_ref)
    gram = jnp.zeros((2 * RANK, 2 * RANK), F32)
    for k in range(N_COL):
        gram = gram + lax.dot_general(
            qr_ref[k], qr_ref[k], (((1,), (1,)), ((), ())), preferred_element_type=F32
        )
    gram = gram[:RANK, :RANK] + ((gram[:RANK, RANK:] + gram[RANK:, :RANK]) + gram[RANK:, RANK:])
    for k in range(N_ROW):
        for q in range(4):
            cols_ref[k, RANK:, 64 * q : 64 * q + 64] = gram[16 * q : 16 * q + 16]

    def some(group, carry):
        load(tiles_ref, tiles, sems, group).wait()
        done = []
        for k in range(GROUP):
            slot = group * GROUP + k
            i = table[0][0, slot] % N_COL
            j = row_offset(table, table[0][1, slot] // N_COL)
            tile = tiles[slot]
            into_cols = jnp.dot(qr_ref[i], tile, preferred_element_type=F32)
            into_rows = lax.dot_general(
                qc_ref[j], tile, (((1,), (1,)), ((), ())), preferred_element_type=F32
            )
            done.append((i, j, into_rows[:RANK] + into_rows[RANK:], into_cols[:RANK] + into_cols[RANK:]))
        for i, j, into_rows, into_cols in done:
            cols_ref[j, :RANK] += into_cols
            rows_ref[i] += into_rows
        return carry

    lax.fori_loop(0, groups_of(table), some, 0)


def product(table, tiles, qr, near, far):
    return call(
        product_body,
        [shape(N_COL, RANK, BLOCK), shape(N_ROW, RANK + 16, BLOCK)],
        [SMEM] * 3 + [HBM] + [VMEM] * 3,
        1_000_000_000,
        8 << 20,
        30,
        scratch=[pltpu.VMEM((N_ROW, 2 * RANK, BLOCK), BF16)] + TILES,
    )(*table, tiles, qr, near, far)


PANEL = 8
PACKED = RANK // 2 + 8


def inverse_factor(gram):
    eye = (
        lax.broadcasted_iota(jnp.int32, (RANK, RANK), 0)
        == lax.broadcasted_iota(jnp.int32, (RANK, RANK), 1)
    ).astype(F32)
    work = jnp.concatenate([gram, eye], axis=1)
    out = []
    for base in range(0, RANK, PANEL):
        rows = [work[p : p + 1, :] for p in range(PANEL)]
        entry = {
            (p, q): jnp.broadcast_to(rows[p][:, base + q : base + q + 1], (1, 2 * RANK))
            for p in range(PANEL)
            for q in range(p, PANEL)
        }
        work = work[PANEL:]
        more = base + PANEL < RANK
        factor = [
            jnp.broadcast_to(work[:, base + p : base + p + 1], work.shape)
            for p in range(PANEL if more else 0)
        ]
        for p in range(PANEL):
            inverse = 1.0 / entry[p, p]
            for q in range(p + 1, PANEL):
                ratio = entry[p, q] * inverse
                rows[q] = rows[q] - ratio * rows[p]
                for r in range(q, PANEL):
                    entry[q, r] = entry[q, r] - ratio * entry[p, r]
            if more:
                factor[p] = factor[p] * inverse
                for q in range(p + 1, PANEL):
                    factor[q] = factor[q] - factor[p] * entry[p, q]
            out.append(lax.rsqrt(entry[p, p]) * rows[p])
        if more:
            for p in range(PANEL):
                work = work - factor[p] * rows[p]
    return jnp.concatenate(out, axis=0)[:, RANK:]


def row_less_col(strict):
    row = lax.broadcasted_iota(jnp.int32, (RANK, RANK), 0)
    col = lax.broadcasted_iota(jnp.int32, (RANK, RANK), 1)
    return row < col if strict else row <= col


def eps_eye():
    same = lax.broadcasted_iota(jnp.int32, (RANK, RANK), 0) == lax.broadcasted_iota(
        jnp.int32, (RANK, RANK), 1
    )
    return jnp.where(same, GRAM_EPS, 0.0).astype(F32)


def dot_t(a, b):
    return lax.dot_general(
        a, b, (((1,), (1,)), ((), ())), precision=HIGHEST, preferred_element_type=F32
    )


def mid2_body(rr_ref, own_ref, a_ref, b_ref, c_ref, p_ref, q_ref, wide_ref, gram_ref):
    parts = (a_ref, b_ref, c_ref)
    total = total_of(rr_ref, own_ref, parts)
    packed = own_ref[0, RANK:]
    for part in parts:
        packed = packed + part[0, RANK:]
    gram = jnp.concatenate([packed[:, 64 * q : 64 * q + 64] for q in range(4)], axis=0)
    inverse = inverse_factor(gram / CELLS + eps_eye())
    normal = jnp.dot(inverse, total, precision=HIGHEST, preferred_element_type=F32)
    p_ref[...] = normal
    rounded = normal.astype(BF16)
    q_ref[...] = rounded
    for k in range(N_COL):
        wide_ref[k] = rounded
    gram_ref[...] = dot_t(normal, normal)


def mid2(rr, own, parts):
    return call(
        mid2_body,
        [
            shape(RANK, BLOCK),
            shape(RANK, BLOCK, dtype=BF16),
            shape(N_COL, RANK, BLOCK, dtype=BF16),
            shape(RANK, RANK),
        ],
        [VMEM] * 5,
        10_000_000,
        2 << 20,
        8,
    )(rr, own, *parts)


def project_body(
    pairs,
    count,
    place,
    tiles_ref,
    qr_ref,
    near_ref,
    far_ref,
    gram_ref,
    out_ref,
    cols_ref,
    qc_ref,
    tiles,
    sems,
):
    table = (pairs, count, place)
    load_all(table, tiles_ref, tiles, sems)
    cols_ref[...] = jnp.zeros_like(cols_ref)
    join(near_ref, far_ref, qc_ref)

    def some(group, carry):
        load(tiles_ref, tiles, sems, group).wait()
        done = []
        for k in range(GROUP):
            slot = group * GROUP + k
            i = table[0][0, slot] % N_COL
            j = row_offset(table, table[0][1, slot] // N_COL)
            done.append((j, jnp.dot(qr_ref[i], tiles[slot], preferred_element_type=F32)))
        for j, into_cols in done:
            cols_ref[j] += into_cols
        return carry

    lax.fori_loop(0, groups_of(table), some, 0)
    form = jnp.zeros((RANK, RANK), F32)
    for k in range(N_ROW):
        high = cols_ref[k].astype(BF16)
        low = (cols_ref[k] - high.astype(F32)).astype(BF16)
        both = lax.dot_general(
            jnp.concatenate([high, low], axis=0),
            qc_ref[k],
            (((1,), (1,)), ((), ())),
            preferred_element_type=F32,
        )
        form = form + (both[:RANK] + both[RANK:])
    gram = gram_ref[...]
    packed = jnp.where(row_less_col(False), form + form.T, gram)
    diagonal = jnp.sum(jnp.where(eps_eye() > 0.0, gram, 0.0), axis=0, keepdims=True)
    both = jnp.concatenate([packed[: RANK // 2], packed[RANK // 2 :]], axis=1)
    tail = jnp.concatenate([diagonal, jnp.zeros((1, RANK), F32)], axis=1)
    out_ref[: RANK // 2] = both
    out_ref[RANK // 2 :] = jnp.broadcast_to(tail, (8, 2 * RANK))


def project(table, tiles, qr, near, far, gram):
    return call(
        project_body,
        shape(PACKED, 2 * RANK),
        [SMEM] * 3 + [HBM] + [VMEM] * 4,
        500_000_000,
        6 << 20,
        30,
        scratch=[pltpu.VMEM((N_ROW, RANK, BLOCK), F32), pltpu.VMEM((N_ROW, RANK, BLOCK), BF16)]
        + TILES,
    )(*table, tiles, qr, near, far, gram)


def finish_body(own_ref, a_ref, b_ref, c_ref, p_ref, basis_ref, form_ref):
    total = sum_of_four(own_ref[...], a_ref[...], b_ref[...], c_ref[...])
    top = total[: RANK // 2]
    packed = jnp.concatenate([top[:, :RANK], top[:, RANK:]], axis=0)
    lower = jnp.where(row_less_col(False), 0.0, packed)
    diagonal = jnp.where(eps_eye() > 0.0, total[RANK // 2 : RANK // 2 + 1, :RANK], 0.0)
    inverse = inverse_factor((lower + lower.T + diagonal) / CELLS + eps_eye())
    basis_ref[...] = jnp.dot(inverse, p_ref[...], precision=HIGHEST, preferred_element_type=F32)
    upper = jnp.where(row_less_col(False), packed, 0.0)
    form = (upper + jnp.where(row_less_col(True), packed, 0.0).T) / CELLS
    form_ref[...] = jnp.dot(
        inverse, dot_t(form, inverse), precision=HIGHEST, preferred_element_type=F32
    )


def sum_of_four(own, one, two, three):
    return (own + two) + (one + three)


def finish(parts, p):
    return call(
        finish_body, [shape(RANK, BLOCK), shape(RANK, RANK)], [VMEM] * 5, 10_000_000, 1 << 20, 6
    )(*parts, p)


def swap(x, axis):
    return lax.all_to_all(x, axis, 0, 0, tiled=True)


def shift(x, axis, k):
    if axis == "x":
        pairs = [(d, (d // 2 + k) % 4 * 2 + d % 2) for d in range(N_ROW)]
    elif axis == "core":
        pairs = [(d, d ^ k) for d in range(N_ROW)]
    elif axis == "y":
        pairs = [(d, (d // 4 + k) % 4 * 4 + d % 4) for d in range(N_COL)]
    else:
        pairs = [(d, d // 4 * 4 + (d + k) % 4) for d in range(N_COL)]
    return lax.ppermute(x, "row" if axis in ("x", "core") else "col", pairs)


def around(x, axis):
    return [x] + [shift(x, axis, k) for k in range(1, 4)]


def both_ways(pieces, axis):
    low, high = jnp.stack(pieces[:2]), jnp.stack(pieces[2:])
    low_up, high_down = shift(low, axis, 1), shift(high, axis, 3)
    high_up, low_down = shift(high, axis, 1), shift(low, axis, 3)
    low_far, high_far = shift(low_up, axis, 1), shift(high_down, axis, 3)
    return [low, high, low_up, high_up, low_far, high_far, low_down, high_down]


def scatter(rows, cols):
    own = cols[:4] + shift(cols[4:], "core", 1)
    parts = [shift(own[k : k + 1], "x", 4 - k) for k in range(1, 4)]
    return swap(rows, "col"), own, parts


def gather(q, wide):
    near = around(q, "x")
    qr = swap(wide, "col")
    near = jnp.stack(near)
    return qr, near, shift(near, "core", 1)


def local(series, lag_weight, start_basis, block_pairs, pair_count):
    row, col = lax.axis_index("row"), lax.axis_index("col")
    place = jnp.stack([row // 2, row % 2, col // 4, col % 4]).astype(jnp.int32)
    table = (block_pairs.reshape(SLOTS, 2).T, pair_count, place)
    first, second, trail = pack(series, start_basis)
    first, second = around(first, "z"), around(second, "y")
    trail = around(trail, "x")
    first, second = both_ways(first, "y"), both_ways(second, "z")
    own = jnp.stack(trail)
    other = shift(own, "core", 1)
    sums, xc = day_sums(own, other)
    tiles, rows, cols = build(table, lag_weight, sums, xc, first, second)
    q1, wide = mid1(*scatter(rows, cols))
    rows, cols = product(table, tiles, *gather(q1, wide))
    p2, q2, wide, gram = mid2(*scatter(rows, cols))
    part = project(table, tiles, *gather(q2, wide), gram)
    part = part + shift(part, "core", 1)
    part = sum_of_four(*around(part, "x"))
    part = sum_of_four(*around(part, "z"))
    return finish(around(part, "y"), p2)


def solution(mesh):
    return jax.shard_map(
        local,
        mesh=mesh,
        in_specs=(
            P(None, ("row", "col")),
            P(),
            P(None, ("row", "col")),
            P("row", "col", None, None),
            P("row", "col"),
        ),
        out_specs=(P(None, ("row", "col")), P()),
        check_vma=False,
    )
```

```python
import jax
import jax.numpy as jnp
from jax import lax
from jax.experimental import pallas as pl
from jax.experimental.pallas import tpu as pltpu
from jax.sharding import PartitionSpec as P


BLOCK = 256
DAYS = 512
LAGS = 4
RANK = 64
SLOTS = 32
N_ROW = 8
N_COL = 16
CELLS = 32768
BETA_CORR = 8.0
GRAM_EPS = 1e-05
TILE_SCALE = 0.25 / 16.0
HIGHEST = lax.Precision.HIGHEST
F32 = jnp.float32
BF16 = jnp.bfloat16
VMEM = pl.BlockSpec(memory_space=pltpu.VMEM)
HBM = pl.BlockSpec(memory_space=pltpu.HBM)
ANY = pl.BlockSpec(memory_space=pl.ANY)
SMEM = pl.BlockSpec(memory_space=pltpu.SMEM)


def call(body, out_shape, in_specs, flops, nbytes, limit, scratch=(), out_specs=None):
    many = isinstance(out_shape, (list, tuple))
    return pl.pallas_call(
        body,
        out_shape=out_shape,
        in_specs=in_specs,
        out_specs=out_specs or ([VMEM] * len(out_shape) if many else VMEM),
        scratch_shapes=list(scratch),
        compiler_params=pltpu.CompilerParams(vmem_limit_bytes=limit << 20),
        cost_estimate=pl.CostEstimate(flops=flops, bytes_accessed=nbytes, transcendentals=0),
    )


def shape(*dims, dtype=F32):
    return jax.ShapeDtypeStruct(dims, dtype)


def pack_body(series_ref, start_ref, first_ref, second_ref, trail_ref):
    trail_ref[:DAYS] = series_ref[...]
    trail_ref[DAYS:] = start_ref[...]
    first_ref[:16, :BLOCK] = start_ref[:16]
    first_ref[:16, BLOCK:] = start_ref[32:48]
    second_ref[BLOCK // 2 :, :BLOCK] = start_ref[16:32]
    second_ref[BLOCK // 2 :, BLOCK:] = start_ref[48:]
    first_ref[16:] = series_ref[:, : BLOCK // 2].T
    second_ref[: BLOCK // 2] = series_ref[:, BLOCK // 2 :].T


def pack(series, start):
    half = shape(BLOCK // 2 + 16, DAYS, dtype=BF16)
    return call(
        pack_body,
        [half, half, shape(DAYS + RANK, BLOCK, dtype=BF16)],
        [VMEM, VMEM],
        100_000,
        1 << 20,
        4,
    )(series, start)


EDGE = 16


def shift_body(own_ref, other_ref, out_ref, xc_ref):
    day = lax.broadcasted_iota(jnp.int32, (EDGE, BLOCK), 0)
    for core, ref in enumerate((own_ref, other_ref)):

        def one(step, carry, core=core, ref=ref):
            block = 4 * core + step
            x = ref[step, :DAYS].astype(F32) * (BETA_CORR / DAYS)
            out_ref[block, 0] = (x + x).astype(BF16)
            for lag in range(1, LAGS):
                later, earlier = pltpu.roll(x, DAYS - lag, 0), pltpu.roll(x, lag, 0)
                total = later + earlier
                head = jnp.where(day < lag, later[:EDGE], total[:EDGE])
                tail = jnp.where(day >= EDGE - lag, earlier[DAYS - EDGE :], total[DAYS - EDGE :])
                total = jnp.concatenate([head, total[EDGE : DAYS - EDGE], tail], axis=0)
                out_ref[block, lag] = total.astype(BF16)
            xc_ref[block] = ref[step, DAYS:]
            return carry

        lax.fori_loop(0, 4, one, 0)


def day_sums(own, other):
    return call(
        shift_body,
        [shape(N_ROW, LAGS, DAYS, BLOCK, dtype=BF16), shape(N_ROW, RANK, BLOCK, dtype=BF16)],
        [VMEM, VMEM],
        10_000_000,
        24 << 20,
        16,
    )(own, other)


HALF = BLOCK // 2
GROUP = 4
TILE_ROOM = 288


def count_of(table):
    return table[1][0, 0]


def row_offset(table, j):
    place = table[2]
    return ((j ^ place[1]) & 1) * 4 + ((place[0] - j // 2) & 3)


def groups_of(table):
    return (count_of(table) + GROUP - 1) // GROUP


def build_body(pairs, count, place, weight, sums_ref, xc_ref, *rest):
    table = (pairs, count, place)
    first, second = rest[:8], rest[8:16]
    tiles_ref, rows_ref, cols_ref, at_ref, buffer, sems, out_sems = rest[16:]
    copies = []

    def fetch(src, dst):
        copies.append(pltpu.make_async_copy(src, dst, sems.at[len(copies)]))
        copies[-1].start()

    for k in range(4):
        for h in range(2):
            two = slice(2 * h, 2 * h + 2)
            a, b = first[2 * k + h], second[2 * k + h]
            fetch(a, at_ref.at[k, two, : HALF + 16])
            fetch(b, at_ref.at[two, k, HALF + 16 :])
    rows_ref[...] = jnp.zeros_like(rows_ref)
    cols_ref[...] = jnp.zeros_like(cols_ref)
    buffer[1] = jnp.zeros((GROUP, BLOCK, BLOCK), BF16)
    for copy in copies:
        copy.wait()
    groups = groups_of(table)

    def indices(slot):
        i = table[0][0, slot] % N_COL
        from_y = (table[2][2] - i // 4) & 3
        from_z = (table[2][3] - i) & 3
        return i, from_y, from_z, row_offset(table, table[0][1, slot] // N_COL)

    def basis_of(from_y, from_z):
        ends = [at_ref[from_y, from_z, :16], at_ref[from_y, from_z, 16 + BLOCK :]]
        return jnp.concatenate([e[:, BLOCK * q : BLOCK * q + BLOCK] for q in range(2) for e in ends], axis=0)

    def products(group, side):
        done = []
        for k in range(GROUP):
            i, from_y, from_z, from_row = indices(GROUP * group + k)
            tile = buffer[side, k]
            into_cols = jnp.dot(basis_of(from_y, from_z), tile, preferred_element_type=F32)
            into_rows = lax.dot_general(
                xc_ref[from_row], tile, (((1,), (1,)), ((), ())), preferred_element_type=F32
            )
            done.append((i, from_row, into_rows, into_cols))
        for i, from_row, into_rows, into_cols in done:
            cols_ref[from_row] += into_cols
            rows_ref[i] += into_rows

    def tile_of(slot):
        _, from_y, from_z, from_row = indices(slot)
        live = jnp.where(slot < count_of(table), TILE_SCALE, 0.0)
        lead = at_ref[from_y, from_z, 16 : 16 + BLOCK]
        total = None
        for lag in range(LAGS):
            lagged = jnp.dot(lead, sums_ref[from_row, lag], preferred_element_type=F32)
            term = weight[lag] * jnp.tanh(lagged)
            total = term if total is None else total + term
        return (total * live).astype(BF16)

    def store(group, side):
        return pltpu.make_async_copy(
            buffer.at[side], tiles_ref.at[pl.ds(GROUP * group, GROUP)], out_sems.at[side]
        )

    def one(group, carry):
        side = group & 1
        products(jnp.maximum(group - 1, 0), 1 - side)
        made = [tile_of(GROUP * group + k) for k in range(GROUP)]

        @pl.when(group >= 2)
        def _():
            store(group - 2, side).wait()

        for k in range(GROUP):
            buffer[side, k] = made[k]
        store(group, side).start()
        return carry

    lax.fori_loop(0, groups, one, 0)
    products(groups - 1, (groups - 1) & 1)

    @pl.when(groups >= 2)
    def _():
        store(groups - 2, groups & 1).wait()

    store(groups - 1, (groups - 1) & 1).wait()


def build(table, weight, sums, xc, first, second):
    return call(
        build_body,
        [
            shape(TILE_ROOM, BLOCK, BLOCK, dtype=BF16),
            shape(N_COL, RANK, BLOCK),
            shape(N_ROW, RANK, BLOCK),
        ],
        [SMEM] * 4 + [VMEM] * 2 + [ANY] * 16,
        9_000_000_000,
        20 << 20,
        30,
        scratch=[
            pltpu.VMEM((4, 4, BLOCK + 32, DAYS), BF16),
            pltpu.VMEM((2, GROUP, BLOCK, BLOCK), BF16),
            pltpu.SemaphoreType.DMA((16,)),
            pltpu.SemaphoreType.DMA((2,)),
        ],
        out_specs=[HBM, VMEM, VMEM],
    )(*table, weight, sums, xc, *first, *second)


def total_of(rr_ref, own_ref, parts):
    total = rr_ref[0] + own_ref[0, :RANK]
    for k in range(1, N_COL):
        total = total + rr_ref[k]
    for part in parts:
        total = total + part[0, :RANK]
    return total


def mid1_body(rr_ref, own_ref, a_ref, b_ref, c_ref, out_ref, wide_ref):
    total = total_of(rr_ref, own_ref, (a_ref, b_ref, c_ref))
    high = total.astype(BF16)
    both = jnp.concatenate([high, (total - high.astype(F32)).astype(BF16)], axis=0)
    out_ref[...] = both
    for k in range(N_COL):
        wide_ref[k] = both


def mid1(rr, own, parts):
    return call(
        mid1_body,
        [shape(2 * RANK, BLOCK, dtype=BF16), shape(N_COL, 2 * RANK, BLOCK, dtype=BF16)],
        [VMEM] * 5,
        1_000_000,
        4 << 20,
        8,
    )(rr, own, *parts)


def load(tiles_ref, tiles, sems, group):
    slots = pl.ds(group * GROUP, GROUP)
    return pltpu.make_async_copy(tiles_ref.at[slots], tiles.at[slots], sems.at[group])


def load_all(table, tiles_ref, tiles, sems):
    def begin(group, carry):
        load(tiles_ref, tiles, sems, group).start()
        return carry

    lax.fori_loop(0, groups_of(table), begin, 0)


TILES = [pltpu.VMEM((SLOTS, BLOCK, BLOCK), BF16), pltpu.SemaphoreType.DMA((SLOTS // GROUP,))]


def join(near_ref, far_ref, joined_ref):
    joined_ref[:4] = near_ref[...]
    joined_ref[4:] = far_ref[...]


def product_body(
    pairs, count, place, tiles_ref, qr_ref, near_ref, far_ref, rows_ref, cols_ref, qc_ref, tiles, sems
):
    table = (pairs, count, place)
    load_all(table, tiles_ref, tiles, sems)
    rows_ref[...] = jnp.zeros_like(rows_ref)
    cols_ref[...] = jnp.zeros_like(cols_ref)
    join(near_ref, far_ref, qc_ref)
    gram = jnp.zeros((2 * RANK, 2 * RANK), F32)
    for k in range(N_COL):
        gram = gram + lax.dot_general(
            qr_ref[k], qr_ref[k], (((1,), (1,)), ((), ())), preferred_element_type=F32
        )
    gram = gram[:RANK, :RANK] + ((gram[:RANK, RANK:] + gram[RANK:, :RANK]) + gram[RANK:, RANK:])
    for k in range(N_ROW):
        for q in range(4):
            cols_ref[k, RANK:, 64 * q : 64 * q + 64] = gram[16 * q : 16 * q + 16]

    def some(group, carry):
        load(tiles_ref, tiles, sems, group).wait()
        done = []
        for k in range(GROUP):
            slot = group * GROUP + k
            i = table[0][0, slot] % N_COL
            j = row_offset(table, table[0][1, slot] // N_COL)
            tile = tiles[slot]
            into_cols = jnp.dot(qr_ref[i], tile, preferred_element_type=F32)
            into_rows = lax.dot_general(
                qc_ref[j], tile, (((1,), (1,)), ((), ())), preferred_element_type=F32
            )
            done.append((i, j, into_rows[:RANK] + into_rows[RANK:], into_cols[:RANK] + into_cols[RANK:]))
        for i, j, into_rows, into_cols in done:
            cols_ref[j, :RANK] += into_cols
            rows_ref[i] += into_rows
        return carry

    lax.fori_loop(0, groups_of(table), some, 0)


def product(table, tiles, qr, near, far):
    return call(
        product_body,
        [shape(N_COL, RANK, BLOCK), shape(N_ROW, RANK + 16, BLOCK)],
        [SMEM] * 3 + [HBM] + [VMEM] * 3,
        1_000_000_000,
        8 << 20,
        30,
        scratch=[pltpu.VMEM((N_ROW, 2 * RANK, BLOCK), BF16)] + TILES,
    )(*table, tiles, qr, near, far)


PANEL = 8
PACKED = RANK // 2 + 8


def inverse_factor(gram):
    eye = (
        lax.broadcasted_iota(jnp.int32, (RANK, RANK), 0)
        == lax.broadcasted_iota(jnp.int32, (RANK, RANK), 1)
    ).astype(F32)
    work = jnp.concatenate([gram, eye], axis=1)
    out = []
    for base in range(0, RANK, PANEL):
        rows = [work[p : p + 1, :] for p in range(PANEL)]
        entry = {
            (p, q): jnp.broadcast_to(rows[p][:, base + q : base + q + 1], (1, 2 * RANK))
            for p in range(PANEL)
            for q in range(p, PANEL)
        }
        work = work[PANEL:]
        more = base + PANEL < RANK
        factor = [
            jnp.broadcast_to(work[:, base + p : base + p + 1], work.shape)
            for p in range(PANEL if more else 0)
        ]
        for p in range(PANEL):
            inverse = 1.0 / entry[p, p]
            for q in range(p + 1, PANEL):
                ratio = entry[p, q] * inverse
                rows[q] = rows[q] - ratio * rows[p]
                for r in range(q, PANEL):
                    entry[q, r] = entry[q, r] - ratio * entry[p, r]
            if more:
                factor[p] = factor[p] * inverse
                for q in range(p + 1, PANEL):
                    factor[q] = factor[q] - factor[p] * entry[p, q]
            out.append(lax.rsqrt(entry[p, p]) * rows[p])
        if more:
            for p in range(PANEL):
                work = work - factor[p] * rows[p]
    return jnp.concatenate(out, axis=0)[:, RANK:]


def row_less_col(strict):
    row = lax.broadcasted_iota(jnp.int32, (RANK, RANK), 0)
    col = lax.broadcasted_iota(jnp.int32, (RANK, RANK), 1)
    return row < col if strict else row <= col


def eps_eye():
    same = lax.broadcasted_iota(jnp.int32, (RANK, RANK), 0) == lax.broadcasted_iota(
        jnp.int32, (RANK, RANK), 1
    )
    return jnp.where(same, GRAM_EPS, 0.0).astype(F32)


def dot_t(a, b):
    return lax.dot_general(
        a, b, (((1,), (1,)), ((), ())), precision=HIGHEST, preferred_element_type=F32
    )


def mid2_body(rr_ref, own_ref, a_ref, b_ref, c_ref, p_ref, q_ref, wide_ref, gram_ref):
    parts = (a_ref, b_ref, c_ref)
    total = total_of(rr_ref, own_ref, parts)
    packed = own_ref[0, RANK:]
    for part in parts:
        packed = packed + part[0, RANK:]
    gram = jnp.concatenate([packed[:, 64 * q : 64 * q + 64] for q in range(4)], axis=0)
    inverse = inverse_factor(gram / CELLS + eps_eye())
    normal = jnp.dot(inverse, total, precision=HIGHEST, preferred_element_type=F32)
    p_ref[...] = normal
    rounded = normal.astype(BF16)
    q_ref[...] = rounded
    for k in range(N_COL):
        wide_ref[k] = rounded
    gram_ref[...] = dot_t(normal, normal)


def mid2(rr, own, parts):
    return call(
        mid2_body,
        [
            shape(RANK, BLOCK),
            shape(RANK, BLOCK, dtype=BF16),
            shape(N_COL, RANK, BLOCK, dtype=BF16),
            shape(RANK, RANK),
        ],
        [VMEM] * 5,
        10_000_000,
        2 << 20,
        8,
    )(rr, own, *parts)


def project_body(
    pairs,
    count,
    place,
    tiles_ref,
    qr_ref,
    near_ref,
    far_ref,
    gram_ref,
    out_ref,
    cols_ref,
    qc_ref,
    tiles,
    sems,
):
    table = (pairs, count, place)
    load_all(table, tiles_ref, tiles, sems)
    cols_ref[...] = jnp.zeros_like(cols_ref)
    join(near_ref, far_ref, qc_ref)

    def some(group, carry):
        load(tiles_ref, tiles, sems, group).wait()
        done = []
        for k in range(GROUP):
            slot = group * GROUP + k
            i = table[0][0, slot] % N_COL
            j = row_offset(table, table[0][1, slot] // N_COL)
            done.append((j, jnp.dot(qr_ref[i], tiles[slot], preferred_element_type=F32)))
        for j, into_cols in done:
            cols_ref[j] += into_cols
        return carry

    lax.fori_loop(0, groups_of(table), some, 0)
    form = jnp.zeros((RANK, RANK), F32)
    for k in range(N_ROW):
        high = cols_ref[k].astype(BF16)
        low = (cols_ref[k] - high.astype(F32)).astype(BF16)
        both = lax.dot_general(
            jnp.concatenate([high, low], axis=0),
            qc_ref[k],
            (((1,), (1,)), ((), ())),
            preferred_element_type=F32,
        )
        form = form + (both[:RANK] + both[RANK:])
    gram = gram_ref[...]
    packed = jnp.where(row_less_col(False), form + form.T, gram)
    diagonal = jnp.sum(jnp.where(eps_eye() > 0.0, gram, 0.0), axis=0, keepdims=True)
    both = jnp.concatenate([packed[: RANK // 2], packed[RANK // 2 :]], axis=1)
    tail = jnp.concatenate([diagonal, jnp.zeros((1, RANK), F32)], axis=1)
    out_ref[: RANK // 2] = both
    out_ref[RANK // 2 :] = jnp.broadcast_to(tail, (8, 2 * RANK))


def project(table, tiles, qr, near, far, gram):
    return call(
        project_body,
        shape(PACKED, 2 * RANK),
        [SMEM] * 3 + [HBM] + [VMEM] * 4,
        500_000_000,
        6 << 20,
        30,
        scratch=[pltpu.VMEM((N_ROW, RANK, BLOCK), F32), pltpu.VMEM((N_ROW, RANK, BLOCK), BF16)]
        + TILES,
    )(*table, tiles, qr, near, far, gram)


def respread_body(own_ref, a_ref, b_ref, c_ref, out_ref):
    total = sum_of_four(own_ref[...], a_ref[...], b_ref[...], c_ref[...])
    for k in range(N_COL):
        out_ref[k] = total


def respread(parts):
    return call(
        respread_body, shape(N_COL, PACKED, 2 * RANK), [VMEM] * 4, 100_000, 1 << 19, 4
    )(*parts)


def finish_body(parts_ref, p_ref, basis_ref, form_ref):
    total = parts_ref[0]
    for k in range(1, N_COL):
        total = total + parts_ref[k]
    top = total[: RANK // 2]
    packed = jnp.concatenate([top[:, :RANK], top[:, RANK:]], axis=0)
    lower = jnp.where(row_less_col(False), 0.0, packed)
    diagonal = jnp.where(eps_eye() > 0.0, total[RANK // 2 : RANK // 2 + 1, :RANK], 0.0)
    inverse = inverse_factor((lower + lower.T + diagonal) / CELLS + eps_eye())
    basis_ref[...] = jnp.dot(inverse, p_ref[...], precision=HIGHEST, preferred_element_type=F32)
    upper = jnp.where(row_less_col(False), packed, 0.0)
    form = (upper + jnp.where(row_less_col(True), packed, 0.0).T) / CELLS
    form_ref[...] = jnp.dot(
        inverse, dot_t(form, inverse), precision=HIGHEST, preferred_element_type=F32
    )


def sum_of_four(own, one, two, three):
    return (own + two) + (one + three)


def finish(parts, p):
    return call(
        finish_body, [shape(RANK, BLOCK), shape(RANK, RANK)], [VMEM] * 2, 10_000_000, 1 << 20, 6
    )(parts, p)


def swap(x, axis):
    return lax.all_to_all(x, axis, 0, 0, tiled=True)


def shift(x, axis, k):
    if axis == "x":
        pairs = [(d, (d // 2 + k) % 4 * 2 + d % 2) for d in range(N_ROW)]
    elif axis == "core":
        pairs = [(d, d ^ k) for d in range(N_ROW)]
    elif axis == "y":
        pairs = [(d, (d // 4 + k) % 4 * 4 + d % 4) for d in range(N_COL)]
    else:
        pairs = [(d, d // 4 * 4 + (d + k) % 4) for d in range(N_COL)]
    return lax.ppermute(x, "row" if axis in ("x", "core") else "col", pairs)


def around(x, axis):
    return [x] + [shift(x, axis, k) for k in range(1, 4)]


def both_ways(pieces, axis):
    low, high = jnp.stack(pieces[:2]), jnp.stack(pieces[2:])
    low_up, high_down = shift(low, axis, 1), shift(high, axis, 3)
    high_up, low_down = shift(high, axis, 1), shift(low, axis, 3)
    low_far, high_far = shift(low_up, axis, 1), shift(high_down, axis, 3)
    return [low, high, low_up, high_up, low_far, high_far, low_down, high_down]


def scatter(rows, cols):
    own = cols[:4] + shift(cols[4:], "core", 1)
    parts = [shift(own[k : k + 1], "x", 4 - k) for k in range(1, 4)]
    return swap(rows, "col"), own, parts


def gather(q, wide):
    near = around(q, "x")
    qr = swap(wide, "col")
    near = jnp.stack(near)
    return qr, near, shift(near, "core", 1)


def local(series, lag_weight, start_basis, block_pairs, pair_count):
    row, col = lax.axis_index("row"), lax.axis_index("col")
    place = jnp.stack([row // 2, row % 2, col // 4, col % 4]).astype(jnp.int32)
    table = (block_pairs.reshape(SLOTS, 2).T, pair_count, place)
    first, second, trail = pack(series, start_basis)
    first, second = around(first, "z"), around(second, "y")
    trail = around(trail, "x")
    first, second = both_ways(first, "y"), both_ways(second, "z")
    own = jnp.stack(trail)
    other = shift(own, "core", 1)
    sums, xc = day_sums(own, other)
    tiles, rows, cols = build(table, lag_weight, sums, xc, first, second)
    q1, wide = mid1(*scatter(rows, cols))
    rows, cols = product(table, tiles, *gather(q1, wide))
    p2, q2, wide, gram = mid2(*scatter(rows, cols))
    part = project(table, tiles, *gather(q2, wide), gram)
    part = part + shift(part, "core", 1)
    return finish(swap(respread(around(part, "x")), "col"), p2)


def solution(mesh):
    return jax.shard_map(
        local,
        mesh=mesh,
        in_specs=(
            P(None, ("row", "col")),
            P(),
            P(None, ("row", "col")),
            P("row", "col", None, None),
            P("row", "col"),
        ),
        out_specs=(P(None, ("row", "col")), P()),
        check_vma=False,
    )
```

```python
import jax
import jax.numpy as jnp
from jax import lax
from jax.experimental import pallas as pl
from jax.experimental.pallas import tpu as pltpu
from jax.sharding import PartitionSpec as P


BLOCK = 256
DAYS = 512
LAGS = 4
RANK = 64
SLOTS = 32
N_ROW = 8
N_COL = 16
CELLS = 32768
BETA_CORR = 8.0
GRAM_EPS = 1e-05
TILE_SCALE = 0.25 / 16.0
HIGHEST = lax.Precision.HIGHEST
F32 = jnp.float32
BF16 = jnp.bfloat16
VMEM = pl.BlockSpec(memory_space=pltpu.VMEM)
HBM = pl.BlockSpec(memory_space=pltpu.HBM)
ANY = pl.BlockSpec(memory_space=pl.ANY)
SMEM = pl.BlockSpec(memory_space=pltpu.SMEM)


def call(body, out_shape, in_specs, flops, nbytes, limit, scratch=(), out_specs=None):
    many = isinstance(out_shape, (list, tuple))
    return pl.pallas_call(
        body,
        out_shape=out_shape,
        in_specs=in_specs,
        out_specs=out_specs or ([VMEM] * len(out_shape) if many else VMEM),
        scratch_shapes=list(scratch),
        compiler_params=pltpu.CompilerParams(vmem_limit_bytes=limit << 20),
        cost_estimate=pl.CostEstimate(flops=flops, bytes_accessed=nbytes, transcendentals=0),
    )


def shape(*dims, dtype=F32):
    return jax.ShapeDtypeStruct(dims, dtype)


def pack_body(series_hbm, start_hbm, first_ref, second_ref, trail_ref, series_ref, start_ref, sems):
    copies = [
        pltpu.make_async_copy(series_hbm, series_ref, sems.at[0]),
        pltpu.make_async_copy(start_hbm, start_ref, sems.at[1]),
    ]
    for copy in copies:
        copy.start()
    for copy in copies:
        copy.wait()
    trail_ref[:DAYS] = series_ref[...]
    trail_ref[DAYS:] = start_ref[...]
    first_ref[:16, :BLOCK] = start_ref[:16]
    first_ref[:16, BLOCK:] = start_ref[32:48]
    second_ref[BLOCK // 2 :, :BLOCK] = start_ref[16:32]
    second_ref[BLOCK // 2 :, BLOCK:] = start_ref[48:]
    first_ref[16:] = series_ref[:, : BLOCK // 2].T
    second_ref[: BLOCK // 2] = series_ref[:, BLOCK // 2 :].T


def pack(series, start):
    half = shape(BLOCK // 2 + 16, DAYS, dtype=BF16)
    return call(
        pack_body,
        [half, half, shape(DAYS + RANK, BLOCK, dtype=BF16)],
        [HBM, HBM],
        100_000,
        1 << 20,
        59,
        scratch=[
            pltpu.VMEM((DAYS, BLOCK), BF16),
            pltpu.VMEM((RANK, BLOCK), BF16),
            pltpu.SemaphoreType.DMA((2,)),
        ],
    )(series, start)


EDGE = 16


def shift_body(own_ref, other_ref, out_ref, xc_ref):
    day = lax.broadcasted_iota(jnp.int32, (EDGE, BLOCK), 0)
    for core, ref in enumerate((own_ref, other_ref)):

        def one(step, carry, core=core, ref=ref):
            block = 4 * core + step
            x = ref[step, :DAYS].astype(F32) * (BETA_CORR / DAYS)
            out_ref[block, 0] = (x + x).astype(BF16)
            for lag in range(1, LAGS):
                later, earlier = pltpu.roll(x, DAYS - lag, 0), pltpu.roll(x, lag, 0)
                total = later + earlier
                head = jnp.where(day < lag, later[:EDGE], total[:EDGE])
                tail = jnp.where(day >= EDGE - lag, earlier[DAYS - EDGE :], total[DAYS - EDGE :])
                total = jnp.concatenate([head, total[EDGE : DAYS - EDGE], tail], axis=0)
                out_ref[block, lag] = total.astype(BF16)
            xc_ref[block] = ref[step, DAYS:]
            return carry

        lax.fori_loop(0, 4, one, 0)


def day_sums(own, other):
    return call(
        shift_body,
        [shape(N_ROW, LAGS, DAYS, BLOCK, dtype=BF16), shape(N_ROW, RANK, BLOCK, dtype=BF16)],
        [VMEM, VMEM],
        10_000_000,
        24 << 20,
        16,
    )(own, other)


HALF = BLOCK // 2
GROUP = 4
TILE_ROOM = 288


def count_of(table):
    return table[1][4]


def row_offset(table, j):
    place = table[1]
    return ((j ^ place[1]) & 1) * 4 + ((place[0] - j // 2) & 3)


def groups_of(table):
    return (count_of(table) + GROUP - 1) // GROUP


def build_body(pairs, place, weight, sums_ref, xc_ref, *rest):
    table = (pairs, place)
    first, second = rest[:8], rest[8:16]
    tiles_ref, rows_ref, cols_ref, at_ref, buffer, sems, out_sems = rest[16:]
    copies = []

    def fetch(src, dst):
        copies.append(pltpu.make_async_copy(src, dst, sems.at[len(copies)]))
        copies[-1].start()

    for k in range(4):
        for h in range(2):
            two = slice(2 * h, 2 * h + 2)
            a, b = first[2 * k + h], second[2 * k + h]
            fetch(a, at_ref.at[k, two, : HALF + 16])
            fetch(b, at_ref.at[two, k, HALF + 16 :])
    rows_ref[...] = jnp.zeros_like(rows_ref)
    cols_ref[...] = jnp.zeros_like(cols_ref)
    buffer[1] = jnp.zeros((GROUP, BLOCK, BLOCK), BF16)
    for copy in copies:
        copy.wait()
    groups = groups_of(table)

    def indices(slot):
        i = table[0][0, slot] % N_COL
        from_y = (table[1][2] - i // 4) & 3
        from_z = (table[1][3] - i) & 3
        return i, from_y, from_z, row_offset(table, table[0][1, slot] // N_COL)

    def basis_of(from_y, from_z):
        ends = [at_ref[from_y, from_z, :16], at_ref[from_y, from_z, 16 + BLOCK :]]
        return jnp.concatenate([e[:, BLOCK * q : BLOCK * q + BLOCK] for q in range(2) for e in ends], axis=0)

    def products(group, side):
        done = []
        for k in range(GROUP):
            i, from_y, from_z, from_row = indices(GROUP * group + k)
            tile = buffer[side, k]
            into_cols = jnp.dot(basis_of(from_y, from_z), tile, preferred_element_type=F32)
            into_rows = lax.dot_general(
                xc_ref[from_row], tile, (((1,), (1,)), ((), ())), preferred_element_type=F32
            )
            done.append((i, from_row, into_rows, into_cols))
        for i, from_row, into_rows, into_cols in done:
            cols_ref[from_row] += into_cols
            rows_ref[i] += into_rows

    def tile_of(slot):
        _, from_y, from_z, from_row = indices(slot)
        live = jnp.where(slot < count_of(table), TILE_SCALE, 0.0)
        lead = at_ref[from_y, from_z, 16 : 16 + BLOCK]
        total = None
        for lag in range(LAGS):
            lagged = jnp.dot(lead, sums_ref[from_row, lag], preferred_element_type=F32)
            term = weight[lag] * jnp.tanh(lagged)
            total = term if total is None else total + term
        return (total * live).astype(BF16)

    def store(group, side):
        return pltpu.make_async_copy(
            buffer.at[side], tiles_ref.at[pl.ds(GROUP * group, GROUP)], out_sems.at[side]
        )

    def one(group, carry):
        side = group & 1
        products(jnp.maximum(group - 1, 0), 1 - side)
        made = [tile_of(GROUP * group + k) for k in range(GROUP)]

        @pl.when(group >= 2)
        def _():
            store(group - 2, side).wait()

        for k in range(GROUP):
            buffer[side, k] = made[k]
        store(group, side).start()
        return carry

    lax.fori_loop(0, groups, one, 0)
    products(groups - 1, (groups - 1) & 1)

    @pl.when(groups >= 2)
    def _():
        store(groups - 2, groups & 1).wait()

    store(groups - 1, (groups - 1) & 1).wait()


def build(table, weight, sums, xc, first, second):
    return call(
        build_body,
        [
            shape(TILE_ROOM, BLOCK, BLOCK, dtype=BF16),
            shape(N_COL, RANK, BLOCK),
            shape(N_ROW, RANK, BLOCK),
        ],
        [SMEM] * 3 + [VMEM] * 2 + [ANY] * 16,
        9_000_000_000,
        20 << 20,
        30,
        scratch=[
            pltpu.VMEM((4, 4, BLOCK + 32, DAYS), BF16),
            pltpu.VMEM((2, GROUP, BLOCK, BLOCK), BF16),
            pltpu.SemaphoreType.DMA((16,)),
            pltpu.SemaphoreType.DMA((2,)),
        ],
        out_specs=[HBM, VMEM, VMEM],
    )(*table, weight, sums, xc, *first, *second)


def total_of(rr_ref, own_ref, parts):
    total = rr_ref[0] + own_ref[0, :RANK]
    for k in range(1, N_COL):
        total = total + rr_ref[k]
    for part in parts:
        total = total + part[0, :RANK]
    return total


def mid1_body(rr_ref, own_ref, a_ref, b_ref, c_ref, out_ref, wide_ref):
    total = total_of(rr_ref, own_ref, (a_ref, b_ref, c_ref))
    high = total.astype(BF16)
    both = jnp.concatenate([high, (total - high.astype(F32)).astype(BF16)], axis=0)
    out_ref[...] = both
    for k in range(N_COL):
        wide_ref[k] = both


def mid1(rr, own, parts):
    return call(
        mid1_body,
        [shape(2 * RANK, BLOCK, dtype=BF16), shape(N_COL, 2 * RANK, BLOCK, dtype=BF16)],
        [VMEM] * 5,
        1_000_000,
        4 << 20,
        8,
    )(rr, own, *parts)


def load(tiles_ref, tiles, sems, group):
    slots = pl.ds(group * GROUP, GROUP)
    return pltpu.make_async_copy(tiles_ref.at[slots], tiles.at[slots], sems.at[group])


def load_all(table, tiles_ref, tiles, sems):
    def begin(group, carry):
        load(tiles_ref, tiles, sems, group).start()
        return carry

    lax.fori_loop(0, groups_of(table), begin, 0)


TILES = [pltpu.VMEM((SLOTS, BLOCK, BLOCK), BF16), pltpu.SemaphoreType.DMA((SLOTS // GROUP,))]


def join(near_ref, far_ref, joined_ref):
    joined_ref[:4] = near_ref[...]
    joined_ref[4:] = far_ref[...]


def product_body(
    pairs, place, tiles_ref, qr_ref, near_ref, far_ref, rows_ref, cols_ref, qc_ref, tiles, sems
):
    table = (pairs, place)
    load_all(table, tiles_ref, tiles, sems)
    rows_ref[...] = jnp.zeros_like(rows_ref)
    cols_ref[...] = jnp.zeros_like(cols_ref)
    join(near_ref, far_ref, qc_ref)
    gram = jnp.zeros((2 * RANK, 2 * RANK), F32)
    for k in range(N_COL):
        gram = gram + lax.dot_general(
            qr_ref[k], qr_ref[k], (((1,), (1,)), ((), ())), preferred_element_type=F32
        )
    gram = gram[:RANK, :RANK] + ((gram[:RANK, RANK:] + gram[RANK:, :RANK]) + gram[RANK:, RANK:])
    for k in range(N_ROW):
        for q in range(4):
            cols_ref[k, RANK:, 64 * q : 64 * q + 64] = gram[16 * q : 16 * q + 16]

    def some(group, carry):
        load(tiles_ref, tiles, sems, group).wait()
        done = []
        for k in range(GROUP):
            slot = group * GROUP + k
            i = table[0][0, slot] % N_COL
            j = row_offset(table, table[0][1, slot] // N_COL)
            tile = tiles[slot]
            into_cols = jnp.dot(qr_ref[i], tile, preferred_element_type=F32)
            into_rows = lax.dot_general(
                qc_ref[j], tile, (((1,), (1,)), ((), ())), preferred_element_type=F32
            )
            done.append((i, j, into_rows[:RANK] + into_rows[RANK:], into_cols[:RANK] + into_cols[RANK:]))
        for i, j, into_rows, into_cols in done:
            cols_ref[j, :RANK] += into_cols
            rows_ref[i] += into_rows
        return carry

    lax.fori_loop(0, groups_of(table), some, 0)


def product(table, tiles, qr, near, far):
    return call(
        product_body,
        [shape(N_COL, RANK, BLOCK), shape(N_ROW, RANK + 16, BLOCK)],
        [SMEM] * 2 + [HBM] + [VMEM] * 3,
        1_000_000_000,
        8 << 20,
        30,
        scratch=[pltpu.VMEM((N_ROW, 2 * RANK, BLOCK), BF16)] + TILES,
    )(*table, tiles, qr, near, far)


PANEL = 8
PACKED = RANK // 2 + 8


def inverse_factor(gram):
    eye = (
        lax.broadcasted_iota(jnp.int32, (RANK, RANK), 0)
        == lax.broadcasted_iota(jnp.int32, (RANK, RANK), 1)
    ).astype(F32)
    work = jnp.concatenate([gram, eye], axis=1)
    out = []
    for base in range(0, RANK, PANEL):
        rows = [work[p : p + 1, :] for p in range(PANEL)]
        entry = {
            (p, q): jnp.broadcast_to(rows[p][:, base + q : base + q + 1], (1, 2 * RANK))
            for p in range(PANEL)
            for q in range(p, PANEL)
        }
        work = work[PANEL:]
        more = base + PANEL < RANK
        factor = [
            jnp.broadcast_to(work[:, base + p : base + p + 1], work.shape)
            for p in range(PANEL if more else 0)
        ]
        for p in range(PANEL):
            inverse = 1.0 / entry[p, p]
            for q in range(p + 1, PANEL):
                ratio = entry[p, q] * inverse
                rows[q] = rows[q] - ratio * rows[p]
                for r in range(q, PANEL):
                    entry[q, r] = entry[q, r] - ratio * entry[p, r]
            if more:
                factor[p] = factor[p] * inverse
                for q in range(p + 1, PANEL):
                    factor[q] = factor[q] - factor[p] * entry[p, q]
            out.append(lax.rsqrt(entry[p, p]) * rows[p])
        if more:
            for p in range(PANEL):
                work = work - factor[p] * rows[p]
    return jnp.concatenate(out, axis=0)[:, RANK:]


def row_less_col(strict):
    row = lax.broadcasted_iota(jnp.int32, (RANK, RANK), 0)
    col = lax.broadcasted_iota(jnp.int32, (RANK, RANK), 1)
    return row < col if strict else row <= col


def eps_eye():
    same = lax.broadcasted_iota(jnp.int32, (RANK, RANK), 0) == lax.broadcasted_iota(
        jnp.int32, (RANK, RANK), 1
    )
    return jnp.where(same, GRAM_EPS, 0.0).astype(F32)


def dot_t(a, b):
    return lax.dot_general(
        a, b, (((1,), (1,)), ((), ())), precision=HIGHEST, preferred_element_type=F32
    )


def mid2_body(rr_ref, own_ref, a_ref, b_ref, c_ref, p_ref, q_ref, wide_ref, gram_ref):
    parts = (a_ref, b_ref, c_ref)
    total = total_of(rr_ref, own_ref, parts)
    packed = own_ref[0, RANK:]
    for part in parts:
        packed = packed + part[0, RANK:]
    gram = jnp.concatenate([packed[:, 64 * q : 64 * q + 64] for q in range(4)], axis=0)
    inverse = inverse_factor(gram / CELLS + eps_eye())
    normal = jnp.dot(inverse, total, precision=HIGHEST, preferred_element_type=F32)
    p_ref[...] = normal
    rounded = normal.astype(BF16)
    q_ref[...] = rounded
    for k in range(N_COL):
        wide_ref[k] = rounded
    gram_ref[...] = dot_t(normal, normal)


def mid2(rr, own, parts):
    return call(
        mid2_body,
        [
            shape(RANK, BLOCK),
            shape(RANK, BLOCK, dtype=BF16),
            shape(N_COL, RANK, BLOCK, dtype=BF16),
            shape(RANK, RANK),
        ],
        [VMEM] * 5,
        10_000_000,
        2 << 20,
        8,
    )(rr, own, *parts)


def project_body(
    pairs,
    place,
    tiles_ref,
    qr_ref,
    near_ref,
    far_ref,
    gram_ref,
    out_ref,
    cols_ref,
    qc_ref,
    tiles,
    sems,
):
    table = (pairs, place)
    load_all(table, tiles_ref, tiles, sems)
    cols_ref[...] = jnp.zeros_like(cols_ref)
    join(near_ref, far_ref, qc_ref)

    def some(group, carry):
        load(tiles_ref, tiles, sems, group).wait()
        done = []
        for k in range(GROUP):
            slot = group * GROUP + k
            i = table[0][0, slot] % N_COL
            j = row_offset(table, table[0][1, slot] // N_COL)
            done.append((j, jnp.dot(qr_ref[i], tiles[slot], preferred_element_type=F32)))
        for j, into_cols in done:
            cols_ref[j] += into_cols
        return carry

    lax.fori_loop(0, groups_of(table), some, 0)
    form = jnp.zeros((RANK, RANK), F32)
    for k in range(N_ROW):
        high = cols_ref[k].astype(BF16)
        low = (cols_ref[k] - high.astype(F32)).astype(BF16)
        both = lax.dot_general(
            jnp.concatenate([high, low], axis=0),
            qc_ref[k],
            (((1,), (1,)), ((), ())),
            preferred_element_type=F32,
        )
        form = form + (both[:RANK] + both[RANK:])
    gram = gram_ref[...]
    packed = jnp.where(row_less_col(False), form + form.T, gram)
    diagonal = jnp.sum(jnp.where(eps_eye() > 0.0, gram, 0.0), axis=0, keepdims=True)
    both = jnp.concatenate([packed[: RANK // 2], packed[RANK // 2 :]], axis=1)
    tail = jnp.concatenate([diagonal, jnp.zeros((1, RANK), F32)], axis=1)
    out_ref[: RANK // 2] = both
    out_ref[RANK // 2 :] = jnp.broadcast_to(tail, (8, 2 * RANK))


def project(table, tiles, qr, near, far, gram):
    return call(
        project_body,
        shape(PACKED, 2 * RANK),
        [SMEM] * 2 + [HBM] + [VMEM] * 4,
        500_000_000,
        6 << 20,
        30,
        scratch=[pltpu.VMEM((N_ROW, RANK, BLOCK), F32), pltpu.VMEM((N_ROW, RANK, BLOCK), BF16)]
        + TILES,
    )(*table, tiles, qr, near, far, gram)


def respread_body(own_ref, a_ref, b_ref, c_ref, out_ref):
    total = sum_of_four(own_ref[...], a_ref[...], b_ref[...], c_ref[...])
    for k in range(N_COL):
        out_ref[k] = total


def respread(parts):
    return call(
        respread_body, shape(N_COL, PACKED, 2 * RANK), [VMEM] * 4, 100_000, 1 << 19, 4
    )(*parts)


def finish_body(parts_ref, p_ref, basis_ref, form_ref):
    total = parts_ref[0]
    for k in range(1, N_COL):
        total = total + parts_ref[k]
    top = total[: RANK // 2]
    packed = jnp.concatenate([top[:, :RANK], top[:, RANK:]], axis=0)
    lower = jnp.where(row_less_col(False), 0.0, packed)
    diagonal = jnp.where(eps_eye() > 0.0, total[RANK // 2 : RANK // 2 + 1, :RANK], 0.0)
    inverse = inverse_factor((lower + lower.T + diagonal) / CELLS + eps_eye())
    basis_ref[...] = jnp.dot(inverse, p_ref[...], precision=HIGHEST, preferred_element_type=F32)
    upper = jnp.where(row_less_col(False), packed, 0.0)
    form = (upper + jnp.where(row_less_col(True), packed, 0.0).T) / CELLS
    form_ref[...] = jnp.dot(
        inverse, dot_t(form, inverse), precision=HIGHEST, preferred_element_type=F32
    )


def sum_of_four(own, one, two, three):
    return (own + two) + (one + three)


def finish(parts, p):
    return call(
        finish_body, [shape(RANK, BLOCK), shape(RANK, RANK)], [VMEM] * 2, 10_000_000, 1 << 20, 6
    )(parts, p)


def swap(x, axis):
    return lax.all_to_all(x, axis, 0, 0, tiled=True)


def shift(x, axis, k):
    if axis == "x":
        pairs = [(d, (d // 2 + k) % 4 * 2 + d % 2) for d in range(N_ROW)]
    elif axis == "core":
        pairs = [(d, d ^ k) for d in range(N_ROW)]
    elif axis == "y":
        pairs = [(d, (d // 4 + k) % 4 * 4 + d % 4) for d in range(N_COL)]
    else:
        pairs = [(d, d // 4 * 4 + (d + k) % 4) for d in range(N_COL)]
    return lax.ppermute(x, "row" if axis in ("x", "core") else "col", pairs)


def around(x, axis):
    return [x] + [shift(x, axis, k) for k in range(1, 4)]


def both_ways(pieces, axis):
    low, high = jnp.stack(pieces[:2]), jnp.stack(pieces[2:])
    low_up, high_down = shift(low, axis, 1), shift(high, axis, 3)
    high_up, low_down = shift(high, axis, 1), shift(low, axis, 3)
    low_far, high_far = shift(low_up, axis, 1), shift(high_down, axis, 3)
    return [low, high, low_up, high_up, low_far, high_far, low_down, high_down]


def scatter(rows, cols):
    own = cols[:4] + shift(cols[4:], "core", 1)
    parts = [shift(own[k : k + 1], "x", 4 - k) for k in range(1, 4)]
    return swap(rows, "col"), own, parts


def gather(q, wide):
    near = around(q, "x")
    qr = swap(wide, "col")
    near = jnp.stack(near)
    return qr, near, shift(near, "core", 1)


def local(series, lag_weight, start_basis, block_pairs, pair_count):
    row, col = lax.axis_index("row"), lax.axis_index("col")
    place = jnp.stack([row // 2, row % 2, col // 4, col % 4, pair_count[0, 0]]).astype(jnp.int32)
    table = (block_pairs.reshape(SLOTS, 2).T, place)
    first, second, trail = pack(series, start_basis)
    first, second = around(first, "z"), around(second, "y")
    trail = around(trail, "x")
    first, second = both_ways(first, "y"), both_ways(second, "z")
    own = jnp.stack(trail)
    other = shift(own, "core", 1)
    sums, xc = day_sums(own, other)
    tiles, rows, cols = build(table, lag_weight, sums, xc, first, second)
    q1, wide = mid1(*scatter(rows, cols))
    rows, cols = product(table, tiles, *gather(q1, wide))
    p2, q2, wide, gram = mid2(*scatter(rows, cols))
    part = project(table, tiles, *gather(q2, wide), gram)
    part = part + shift(part, "core", 1)
    return finish(swap(respread(around(part, "x")), "col"), p2)


def solution(mesh):
    return jax.shard_map(
        local,
        mesh=mesh,
        in_specs=(
            P(None, ("row", "col")),
            P(),
            P(None, ("row", "col")),
            P("row", "col", None, None),
            P("row", "col"),
        ),
        out_specs=(P(None, ("row", "col")), P()),
        check_vma=False,
    )
```
